256 devices in a mesh: lat: 16 (over z, core), lon: 16 (over x, y).
Axes of the slice: x: 4, y: 4, z: 8, core: 2. Of those that a mesh axis runs over, the one named last changes fastest.
Arguments:
- ensemble: float32 [3, 80, 512, 2048], P(None, None, 'lat', 'lon'), may hold values from -6 to 6
- courant_cols: float32 [1, 512, 2048], P(None, 'lat', 'lon'), may hold values from -0.6 to 0.6
- courant_rows: float32 [1, 512, 2048], P(None, 'lat', 'lon'), may hold values from -0.6 to 0.6
- obs_value: float32 [2, 6144], P(None, ('lat', 'lon')), may hold values from -8 to 8
- obs_error: float32 [2, 6144], P(None, ('lat', 'lon')), may hold values from 0.2 to 2
- obs_cell: int32 [2, 6144], P(None, ('lat', 'lon')), may hold values from 0 to 4095
- obs_kind: int32 [2, 6144], P(None, ('lat', 'lon')), may hold values from 0 to 2
- obs_live: int32 [2, 6144], P(None, ('lat', 'lon')), may hold values from 0 to 1, as said below
- obs_list: int32 [2, 6144, 9], P(None, ('lat', 'lon')), may hold values 0 or 1
Outputs:
- analysis: float32 [3, 80, 512, 2048], P(None, None, 'lat', 'lon')
The draws below stay inside these ranges and needn't reach their ends.
Inputs may be any that keep to these rules, and one draw needn't show every extreme that they name: `obs_live`: in each batch the live slots of a tile are its first ones, and in every batch some tile has all 24 slots live.
All inputs are finite; a program needn't handle non-finite values. No bound on the sum of `obs_list` on one device may be relied on, other than what follows from the above.
Results may differ from the reference program's by a relative error of at most 0.0003.
Values sent between devices are 32-bit elements; how exact they have to be, the bound alone decides.
No kernel may reach another device: no remote copies, remote signals or barrier semaphores. Data moves between devices by JAX's collectives and lax.ppermute only.
A program may use at most 64 MiB of HBM per device.

```python
import math
import jax
import jax.numpy as jnp
from jax import lax

MEMBERS = 80
LEVELS = 1
FIELD_LEVELS = 3
TILE_ROWS = 32
TILE_COLS = 128
OBS_TILE = 24
GRID_ROWS = 512
GRID_COLS = 2048
OBS_SLOTS = 6144
N_LAT = 16
N_LON = 16


def draw_obs_live(key, part):
    first, second, third = jax.random.split(key, 3)
    tiles = OBS_SLOTS // OBS_TILE
    count_a = jax.random.randint(first, (2, tiles), 1, OBS_TILE + 1)
    count_b = jax.random.randint(second, (2, tiles), 1, OBS_TILE + 1)
    counts = jnp.maximum(count_a, count_b)
    fullest = jax.random.randint(third, (2,), 0, tiles)
    counts = jnp.where(jnp.arange(tiles)[None, :] == fullest[:, None], OBS_TILE, counts)
    live = (jnp.arange(OBS_TILE)[None, None, :] < counts[:, :, None]).astype(jnp.int32)
    return live.reshape(2, OBS_SLOTS)


def plant(values, rng, low, largest):
    extent = values.shape
    index_at = [jax.random.randint(jax.random.fold_in(rng, axis), (), 0, extent[axis]) for axis in range(len(extent))]
    values = values.at[tuple(index_at)].set(low)
    longest = extent.index(max(extent))
    index_at[longest] = (index_at[longest] + 1) % extent[longest]
    return values.at[tuple(index_at)].set(largest)


def levels(rng, shape, shards, least, high):
    level = 1.0
    for dim, shards_of in shards:
        steps = jax.random.uniform(jax.random.fold_in(jax.random.fold_in(rng, 6), dim), (shards_of,), jnp.float32, least / len(shards), high / len(shards))
        level = level * jnp.repeat(jnp.exp(steps), shape[dim] // shards_of).reshape((-1,) + (1,) * (len(shape) - 1 - dim))
    return level


def normal_values(own_key, extent, scale, bound, cuts=(), kind=jnp.bfloat16):
    factor_of = levels(own_key, extent, cuts, -0.22, 0.18) if cuts else 1.0
    values = jax.random.normal(own_key, extent, jnp.float32) * scale * factor_of
    return jnp.minimum(jnp.maximum(values, -bound), bound).astype(kind)


def setup_inputs(seed: int = 0) -> dict:
    key_of = jax.random.split(jax.random.key(seed), 10)
    ensemble = normal_values(key_of[0], (FIELD_LEVELS, MEMBERS, GRID_ROWS, GRID_COLS), 1.0, 6.0, ((2, 16), (3, 16)), jnp.float32)
    courant_cols = jnp.clip(jax.random.uniform(key_of[1], (LEVELS, GRID_ROWS, GRID_COLS), jnp.float32, -0.6, 0.6) * levels(key_of[1], (LEVELS, GRID_ROWS, GRID_COLS), ((1, 16), (2, 16)), -0.4, 0.0), -0.6, 0.6)
    courant_rows = jnp.clip(jax.random.uniform(key_of[2], (LEVELS, GRID_ROWS, GRID_COLS), jnp.float32, -0.6, 0.6) * levels(key_of[2], (LEVELS, GRID_ROWS, GRID_COLS), ((1, 16), (2, 16)), -0.4, 0.0), -0.6, 0.6)
    obs_value = normal_values(key_of[3], (2, OBS_SLOTS), 1.5, 8.0, ((1, 256),), jnp.float32)
    obs_error = jnp.clip(jnp.exp(math.log(2.0) - 2.3025851 * jax.random.uniform(key_of[4], (2, OBS_SLOTS), jnp.float32) ** levels(key_of[4], (2, OBS_SLOTS), ((1, 256),), -0.2, 0.2)), 0.2, 2.0)
    obs_cell = plant(jax.random.randint(key_of[5], (2, OBS_SLOTS), 0, TILE_ROWS * TILE_COLS), jax.random.fold_in(key_of[5], 1), 0, (TILE_ROWS * TILE_COLS) - 1).astype(jnp.int32)
    obs_kind = plant(jax.random.randint(key_of[6], (2, OBS_SLOTS), 0, FIELD_LEVELS), jax.random.fold_in(key_of[6], 1), 0, FIELD_LEVELS - 1).astype(jnp.int32)
    obs_live = draw_obs_live(jax.random.fold_in(key_of[9], 71), 0)
    obs_list = plant((jax.random.randint(key_of[8], (2, OBS_SLOTS, 9), 0, 4) < 3).astype(jnp.int32), jax.random.fold_in(key_of[8], 1), 0, 1)
    return {"ensemble": ensemble, "courant_cols": courant_cols, "courant_rows": courant_rows, "obs_value": obs_value, "obs_error": obs_error, "obs_cell": obs_cell, "obs_kind": obs_kind, "obs_live": obs_live, "obs_list": obs_list}


def taper(dist):
    return jnp.square(jnp.maximum(0.0, 1.0 - jnp.abs(dist)))

def advect(state, courant_cols, courant_rows):
    speed_c = jnp.tile(courant_cols, (3, 1, 1))[:, None]
    speed_r = jnp.tile(courant_rows, (3, 1, 1))[:, None]
    padded = jnp.pad(state, ((0, 0), (0, 0), (1, 1), (1, 1)))
    north = padded[:, :, 2:, 1:-1]
    south = padded[:, :, :-2, 1:-1]
    east = padded[:, :, 1:-1, 2:]
    west = padded[:, :, 1:-1, :-2]
    result = state - 0.5 * speed_c * (east - west) + 0.5 * speed_c * speed_c * (east - 2.0 * state + west)
    result = result - 0.5 * speed_r * (north - south) + 0.5 * speed_r * speed_r * (north - 2.0 * state + south)
    return result

def make_table(prior, value, error, live, row_local, col_local, listed):
    members = prior.shape[1]
    ybar = lax.optimization_barrier(jnp.mean(prior, axis=1))
    yperts = prior - ybar[:, None]
    spread = lax.optimization_barrier(jnp.sum(yperts * yperts, axis=1)) / (members - 1)
    total = spread + error
    gain = live.astype(jnp.float32) / total
    alpha = 1.0 / (1.0 + jnp.sqrt(error / total))
    innov = value - ybar
    extra = jnp.stack([gain, innov, alpha, row_local.astype(jnp.float32), col_local.astype(jnp.float32)], axis=1)
    return jnp.concatenate([yperts, extra, listed.astype(jnp.float32)], axis=1)

def assimilate(block, nearby):
    fields, members, trows, tcols = block.shape
    capacity = nearby.shape[2]
    radius = float(trows)
    mean = lax.optimization_barrier(jnp.mean(block, axis=1))
    perts = block - mean[:, None]
    yperts = nearby[:, :, :, :members]
    gain = nearby[:, :, :, members]
    innov = nearby[:, :, :, members + 1]
    alpha = nearby[:, :, :, members + 2]
    orow = nearby[:, :, :, members + 3]
    ocol = nearby[:, :, :, members + 4]
    listed = nearby[:, :, :, members + 5:members + 14]
    offset = jnp.arange(3, dtype=jnp.int32)
    offset_f = offset.astype(jnp.float32) - 1.0
    rows_rel = offset_f[:, None, None] * trows + orow
    cols_rel = offset_f[None, :, None] * tcols + ocol
    slot_of = (2 - offset)[:, None] * 3 + (2 - offset)[None, :]
    onehot = (jnp.arange(9, dtype=jnp.int32)[None, None, :] == slot_of[:, :, None]).astype(jnp.float32)
    chosen = lax.optimization_barrier(jnp.sum(listed * onehot[:, :, None, :], axis=3))
    factor = gain * chosen
    lat_w = taper((rows_rel[..., None] - jnp.arange(trows, dtype=jnp.float32)) / radius) * factor[..., None]
    lon_w = taper((cols_rel[..., None] - jnp.arange(tcols, dtype=jnp.float32)) / radius)
    count = 9 * capacity
    lat_w = lat_w.reshape(count, trows)
    lon_w = lon_w.reshape(count, tcols)
    yperts = yperts.reshape(count, members)
    innov = innov.reshape(count)
    alpha = alpha.reshape(count)
    hi = lax.Precision.HIGHEST
    proj = jnp.einsum('fmij,km->fkij', perts, yperts, precision=hi) / (members - 1)
    weights = proj * lat_w[None, :, :, None] * lon_w[None, :, None, :]
    mean = mean + jnp.einsum('fkij,k->fij', weights, innov, precision=hi)
    perts = perts - jnp.einsum('fkij,km->fmij', weights, alpha[:, None] * yperts, precision=hi)
    return mean[:, None] + perts

def reference(ensemble, courant_cols, courant_rows, obs_value, obs_error, obs_cell, obs_kind, obs_live, obs_list):
    state = advect(ensemble, courant_cols, courant_rows)
    slots = jnp.arange(OBS_SLOTS, dtype=jnp.int32)
    owner = slots // OBS_TILE
    owner_row = owner // N_LON
    owner_col = owner % N_LON
    zero = jnp.zeros((), jnp.int32)
    for batch in range(2):
        row_local = obs_cell[batch] // TILE_COLS
        col_local = obs_cell[batch] % TILE_COLS
        prior = state[obs_kind[batch], :, owner_row * TILE_ROWS + row_local, owner_col * TILE_COLS + col_local]
        table = make_table(prior, obs_value[batch], obs_error[batch], obs_live[batch], row_local, col_local, obs_list[batch])
        width_t = table.shape[1]
        board = jnp.pad(table.reshape(N_LAT, N_LON, OBS_TILE, width_t), ((1, 1), (1, 1), (0, 0), (0, 0)))
        current = state

        def one_tile(tile):
            tile_r = (tile // N_LON).astype(jnp.int32)
            tile_c = (tile % N_LON).astype(jnp.int32)
            nearby = lax.dynamic_slice(board, (tile_r, tile_c, zero, zero), (3, 3, OBS_TILE, width_t))
            block = lax.dynamic_slice(current, (zero, zero, tile_r * TILE_ROWS, tile_c * TILE_COLS), (FIELD_LEVELS, MEMBERS, TILE_ROWS, TILE_COLS))
            return assimilate(block, nearby)
        tiles = lax.map(one_tile, jnp.arange(N_LAT * N_LON, dtype=jnp.int32))
        tiles = tiles.reshape(N_LAT, N_LON, FIELD_LEVELS, MEMBERS, TILE_ROWS, TILE_COLS)
        state = tiles.transpose(2, 3, 0, 4, 1, 5).reshape(FIELD_LEVELS, MEMBERS, GRID_ROWS, GRID_COLS)
    return state
```

```python
import jax
import jax.numpy as jnp
from jax import lax
from jax.experimental import pallas as pl
from jax.experimental.pallas import tpu as pltpu
from jax.sharding import PartitionSpec as P

F, M, R, C, K = 3, 80, 32, 128, 24
GAIN, INNOV, ALPHA, ROW, COL, LIST = 80, 81, 82, 83, 84, 96
S = 80
f32, bf16 = jnp.float32, jnp.bfloat16
VMEM = pltpu.VMEM
MiB = 1 << 20


def lanes(shape):
    return lax.broadcasted_iota(jnp.int32, shape, len(shape) - 1)


def split(x):
    hi = x.astype(bf16)
    return hi, (x - hi.astype(f32)).astype(bf16)


def split3(x):
    hi = x.astype(bf16)
    rest = x - hi.astype(f32)
    mid = rest.astype(bf16)
    return hi, mid, (rest - mid.astype(f32)).astype(bf16)


def dot(a, b, dims=((1,), (0,))):
    return lax.dot_general(a, b, (dims, ((), ())), preferred_element_type=f32)


def edges_kernel(par, x_hbm, xt, row_a, row_b, col_a, col_b, buf, acc, sem):
    for ib in range(R // 8):
        for f in range(F):
            pltpu.make_async_copy(
                x_hbm.at[f, :, pl.ds(ib * 8, 8), :], buf.at[ib, f], sem.at[ib, f]
            ).start()
    acc[...] = jnp.zeros_like(acc)
    lane = lanes((M, C))
    for ib in range(R // 8):
        for f in range(F):
            pltpu.make_async_copy(
                x_hbm.at[f, :, pl.ds(ib * 8, 8), :], buf.at[ib, f], sem.at[ib, f]
            ).wait()
            rows = buf.at[ib, f].reshape(M * 8, C)
            first, last = acc[0], acc[1]
            for r in range(8):
                v = rows[pl.ds(r, M, stride=8), :]
                i = ib * 8 + r
                k = f * R + i
                xt[f, i] = v
                turned = pltpu.roll(v, k, 1) if k else v
                first = jnp.where(lane == k, turned, first)
                last = jnp.where(lane == (k - 1) % C, turned, last)
            acc[0] = first
            acc[1] = last
    first, last = acc[0], pltpu.roll(acc[1], 1, 1)
    odd = (jnp.zeros((M, C), jnp.int32) + par[1]) == 1
    col_a[...] = jnp.where(odd, first, last)
    col_b[...] = jnp.where(odd, last, first)
    ra = jnp.where(par[0] == 1, 0, R - 1)
    rb = R - 1 - ra
    for f in range(F):
        row_a[f] = xt[f, ra]
        row_b[f] = xt[f, rb]


def observe(b, state, cell, kind, value, error, live, listed, table):
    lane = lanes((M, C))
    prior = jnp.zeros((M, C), f32)
    lane1 = lanes((1, C))
    row = jnp.zeros((1, C), f32)
    col = jnp.zeros((1, C), f32)
    for s in range(K):
        at = cell[b, s]
        r, c = at // C, at % C
        v = state[kind[b, s], r]
        prior = jnp.where(lane == s, pltpu.roll(v, (s + C - c) % C, 1), prior)
        row = jnp.where(lane1 == s, r.astype(f32), row)
        col = jnp.where(lane1 == s, c.astype(f32), col)
    ybar = jnp.sum(prior, axis=0, keepdims=True) / M
    yp = prior - ybar
    spread = jnp.sum(yp * yp, axis=0, keepdims=True) / (M - 1)
    err = error[b : b + 1, :]
    total = spread + err
    gain = live[b : b + 1, :] / total
    alpha = 1.0 / (1.0 + jnp.sqrt(err / total))
    innov = value[b : b + 1, :] - ybar
    sub = lax.broadcasted_iota(jnp.int32, (16, C), 0)
    extra = jnp.zeros((16, C), f32)
    for n, v in enumerate((gain, innov, alpha, row, col)):
        extra = jnp.where(sub == n, v, extra)
    whole = jnp.concatenate([yp, extra, jnp.zeros((32, C), f32)], axis=0)
    table[...] = whole.T[:K] + listed[b]


def advect_kernel(
    par, cell, kind, xt, row_a, row_b, col_a, col_b, cc, cr, value, error, live, listed,
    state, table, merged,
):
    lane = lanes((M, C))
    odd_lane = (lane % 2) == 1
    odd_b = (jnp.zeros((M, C), jnp.int32) + par[1]) == 1
    got_a, got_b = col_a[...], col_b[...]
    east = pltpu.roll(jnp.where(odd_b, got_b, got_a), C - 1, 1)
    west = jnp.where(odd_b, got_a, got_b)
    merged[0] = jnp.where(odd_lane, east, west)
    merged[1] = jnp.where(odd_lane, west, east)
    odd_a = (jnp.zeros((M, C), jnp.int32) + par[0]) == 1

    def one(i, parity, low, high):
        u = cc[0, pl.ds(i, 1), :]
        v = cr[0, pl.ds(i, 1), :]
        uu, vv = 0.5 * u * u, 0.5 * v * v
        here = 1.0 - 2.0 * uu - 2.0 * vv
        ae, aw = uu - 0.5 * u, uu + 0.5 * u
        an, as_ = vv - 0.5 * v, vv + 0.5 * v
        for f in range(F):
            x = xt[f, i]
            k = f * R + i
            halo = pltpu.roll(merged[parity], (C - k) % C, 1)
            xe = jnp.where(lane == C - 1, halo, pltpu.roll(x, C - 1, 1))
            xw = jnp.where(lane == 0, halo, pltpu.roll(x, 1, 1))
            if low:
                xs = jnp.where(odd_a, row_a[f], row_b[f])
            else:
                xs = xt[f, i - 1]
            if high:
                xn = jnp.where(odd_a, row_b[f], row_a[f])
            else:
                xn = xt[f, i + 1]
            state[f, i] = here * x + ae * xe + aw * xw + an * xn + as_ * xs

    one(0, 0, True, False)
    one(R - 1, 1, False, True)

    def body(n, carry):
        one(2 * n + 1, 1, False, False)
        one(2 * n + 2, 0, False, False)
        return carry

    lax.fori_loop(0, R // 2 - 1, body, 0)
    observe(0, state, cell, kind, value, error, live, listed, table)


def gather_tables(par, own, side_a, side_b, full):
    sa = 1 - 2 * par[0]
    sb = 1 - 2 * par[1]
    lane = lanes((K, C))
    actives = []
    for q, src in enumerate((own, side_a, side_b)):
        db = (0, sb, -sb)[q]
        for p in range(3):
            da = (0, sa, -sa)[p]
            t = src[pl.ds(p * K, K), :]
            slot = LIST + (1 - da) * 3 + (1 - db)
            chosen = jnp.sum(jnp.where(lane == slot, t, 0.0), axis=1, keepdims=True)
            factor = t[:, GAIN : GAIN + 1] * chosen
            row = t[:, ROW : ROW + 1] + jnp.asarray(da * R, f32)
            col = t[:, COL : COL + 1] + jnp.asarray(db * C, f32)
            t = jnp.where(lane == GAIN, factor, t)
            t = jnp.where(lane == ROW, row, t)
            t = jnp.where(lane == COL, col, t)
            n = (q * 3 + p) * K
            full[n : n + K, :] = t
            near = (row > -float(R)) & (row < 2.0 * R - 1.0) & (col > -float(R)) & (col < C + R - 1.0)
            actives.append(jnp.where(near & (factor != 0.0), 1.0, 0.0))
    return jnp.concatenate(actives, axis=0)


def spread_lanes(hi, lo):
    r = lax.broadcasted_iota(jnp.int32, (C, 2 * C), 0)
    c = lax.broadcasted_iota(jnp.int32, (C, 2 * C), 1)
    keep = r < S
    e_hi = (((c == r) | (c == r + 2 * S)) & keep).astype(f32).astype(bf16)
    e_lo = ((c == r + S) & keep).astype(f32).astype(bf16)
    return (dot(hi, e_hi) + dot(lo, e_lo)).astype(bf16)


def compact(active, full, chunk, ycat, bcat, col_w, row_b, fac_b):
    n = 9 * K
    act = jnp.broadcast_to(active, (n, C))
    tri = (
        lax.broadcasted_iota(jnp.int32, (n, n), 1) < lax.broadcasted_iota(jnp.int32, (n, n), 0)
    ).astype(f32).astype(bf16)
    rank = dot(tri, act.astype(bf16)).astype(jnp.int32) - chunk * S
    lane = lanes((n, C))
    pick = ((rank == lane) & (act > 0.0) & (lane < S)).astype(f32).astype(bf16)
    parts = split3(full[...])
    over = ((0,), (0,))
    chosen = sum(dot(pick, t, over) for t in parts)[:S]
    turned = sum(dot(t, pick, over) for t in parts)
    ycat[...] = spread_lanes(*split(chosen))
    back = turned[INNOV : INNOV + 1, :] - turned[ALPHA : ALPHA + 1, :] * turned[:M]
    bcat[...] = spread_lanes(*split(back))
    col = jnp.broadcast_to(chosen[:, COL : COL + 1], (S, C))
    row_b[...] = jnp.broadcast_to(chosen[:, ROW : ROW + 1], (S, C))
    fac_b[...] = jnp.broadcast_to(chosen[:, GAIN : GAIN + 1], (S, C)) / (M - 1)
    z = jnp.maximum(0.0, 1.0 - jnp.abs(col - lanes((S, C)).astype(f32)) / R)
    col_w[...] = z * z


def localize(i, col_w, row_b, fac_b):
    z = jnp.maximum(0.0, 1.0 - jnp.abs(row_b[...] - i.astype(f32)) / R)
    return z * z * fac_b[...] * col_w[...]


def update(p, lw, ycat, bcat):
    hi, lo = split(p)
    proj = dot(ycat[...], jnp.concatenate([hi, hi, lo, jnp.zeros((16, 2 * C), bf16)], axis=0))
    hi, lo = split(proj * lw)
    return dot(bcat[...], jnp.concatenate([hi, hi, lo, jnp.zeros((16, 2 * C), bf16)], axis=0))


def assimilate(par, own, side_a, side_b, state, scratch, emit, gather_base):
    full, ycat, bcat, col_w, row_b, fac_b, total = scratch
    active = gather_tables(par, own, side_a, side_b, full)
    count = jnp.sum(active).astype(jnp.int32)

    def sweep(base, put):
        def body(n, carry):
            i = 2 * n
            lw = jnp.concatenate(
                [localize(i, col_w, row_b, fac_b), localize(i + 1, col_w, row_b, fac_b)], axis=1
            )
            for f in range(F):
                p = jnp.concatenate([state[f, i], state[f, i + 1]], axis=1)
                d = update(p, lw, ycat, bcat)
                put(n, f, base[f, i] + d[:, :C], base[f, i + 1] + d[:, C:])
            return carry

        return body

    def keep(n, f, a, b):
        total[f, 2 * n] = a
        total[f, 2 * n + 1] = b

    compact_args = (ycat, bcat, col_w, row_b, fac_b)

    @pl.when(count > S)
    def _():
        def chunk(j, carry):
            compact(active, full, j, *compact_args)

            @pl.when(j == 1)
            def _():
                lax.fori_loop(0, R // 2, sweep(state, keep), 0)

            @pl.when(j > 1)
            def _():
                lax.fori_loop(0, R // 2, sweep(total, keep), 0)

            return carry

        lax.fori_loop(1, (count + S - 1) // S, chunk, 0)
        compact(active, full, 0, *compact_args)
        emit(sweep, total)

    @pl.when(count <= S)
    def _():
        compact(active, full, 0, *compact_args)
        emit(sweep, state)


def first_kernel(
    par, cell, kind, own, side_a, side_b, state, value, error, live, listed, out, table, *scratch
):
    def emit(sweep, base):
        def put(n, f, a, b):
            out[f, 2 * n] = a
            out[f, 2 * n + 1] = b

        lax.fori_loop(0, R // 2, sweep(base, put), 0)

    assimilate(par, own, side_a, side_b, state, scratch, emit, None)
    observe(1, out, cell, kind, value, error, live, listed, table)


def second_kernel(par, own, side_a, side_b, state, out, *rest):
    buf, sem, scratch = rest[0], rest[1], rest[2:]

    def copy(ib, f):
        return pltpu.make_async_copy(
            buf.at[ib, f], out.at[f, :, pl.ds(ib * 8, 8), :], sem.at[ib, f]
        )

    def emit(sweep, base):
        for ib in range(R // 8):

            def put(n, f, a, b):
                rows = buf.at[ib, f].reshape(M * 8, C)
                r = 2 * (n - 4 * ib)
                rows[pl.ds(r, M, stride=8), :] = a
                rows[pl.ds(r + 1, M, stride=8), :] = b

            lax.fori_loop(4 * ib, 4 * ib + 4, sweep(base, put), 0)
            for f in range(F):
                copy(ib, f).start()

    assimilate(par, own, side_a, side_b, state, scratch, emit, None)
    for ib in range(R // 8):
        for f in range(F):
            copy(ib, f).wait()


def spec(space):
    return pl.BlockSpec(memory_space=space)


def call(kernel, outs, args, spaces, out_spaces, scratch, name):
    return pl.pallas_call(
        kernel,
        out_shape=outs,
        in_specs=[spec(s) for s in spaces],
        out_specs=[spec(s) for s in out_spaces],
        scratch_shapes=scratch,
        compiler_params=pltpu.CompilerParams(vmem_limit_bytes=40 * MiB),
        name=name,
    )(*args)


def swap(x, axis, shift):
    n = lax.axis_size(axis)
    pairs = [(i, ((i - shift) ^ 1) + shift) for i in range(n)]
    pairs = [(i, j) for i, j in pairs if i >= shift and 0 <= j < n]
    return lax.ppermute(x, axis, pairs)


def on_device(
    ensemble, courant_cols, courant_rows, obs_value, obs_error, obs_cell, obs_kind, obs_live, obs_list
):
    par = jnp.stack([lax.axis_index("lat") % 2, lax.axis_index("lon") % 2]).astype(jnp.int32)
    pad = ((0, 0), (0, C - K))
    value = jnp.pad(obs_value, pad)
    error = jnp.pad(obs_error, pad, constant_values=1.0)
    live = jnp.pad(obs_live.astype(f32), pad)
    listed = jnp.pad(obs_list.astype(f32), ((0, 0), (0, 0), (LIST, C - LIST - 9)))
    SM, HBM = pltpu.SMEM, pltpu.HBM
    block = VMEM((F, R, M, C), f32)
    sds = jax.ShapeDtypeStruct
    table_shape = sds((K, C), f32)

    xt, row_a, row_b, col_a, col_b = call(
        edges_kernel,
        [block, sds((F, M, C), f32), sds((F, M, C), f32), sds((M, C), f32), sds((M, C), f32)],
        [par, ensemble],
        [SM, HBM],
        [VMEM] * 5,
        [VMEM((R // 8, F, M, 8, C), f32), VMEM((2, M, C), f32), pltpu.SemaphoreType.DMA((R // 8, F))],
        "edges",
    )
    row_a, row_b = swap(row_a, "lat", 0), swap(row_b, "lat", 1)
    col_a, col_b = swap(col_a, "lon", 0), swap(col_b, "lon", 1)
    state, table = call(
        advect_kernel,
        [block, table_shape],
        [par, obs_cell, obs_kind, xt, row_a, row_b, col_a, col_b, courant_cols, courant_rows,
         value, error, live, listed],
        [SM] * 3 + [VMEM] * 11,
        [VMEM] * 2,
        [VMEM((2, M, C), f32)],
        "advect",
    )

    def exchange(table):
        own = jnp.concatenate([table, swap(table, "lat", 0), swap(table, "lat", 1)], axis=0)
        return own, swap(own, "lon", 0), swap(own, "lon", 1)

    scratch = [
        VMEM((9 * K, C), f32),
        VMEM((S, 2 * C), bf16),
        VMEM((M, 2 * C), bf16),
        VMEM((S, C), f32),
        VMEM((S, C), f32),
        VMEM((S, C), f32),
        VMEM((F, R, M, C), f32),
    ]
    state, table = call(
        first_kernel,
        [block, table_shape],
        [par, obs_cell, obs_kind, *exchange(table), state, value, error, live, listed],
        [SM] * 3 + [VMEM] * 8,
        [VMEM] * 2,
        scratch,
        "first",
    )
    return call(
        second_kernel,
        [sds((F, M, R, C), f32)],
        [par, *exchange(table), state],
        [SM] + [VMEM] * 4,
        [HBM],
        [VMEM((R // 8, F, M, 8, C), f32), pltpu.SemaphoreType.DMA((R // 8, F))] + scratch,
        "second",
    )[0]


def solution(mesh):
    tiles = P(None, ("lat", "lon"))
    placed = (
        P(None, None, "lat", "lon"),
        P(None, "lat", "lon"),
        P(None, "lat", "lon"),
        tiles,
        tiles,
        tiles,
        tiles,
        tiles,
        P(None, ("lat", "lon"), None),
    )
    return jax.shard_map(
        on_device,
        mesh=mesh,
        in_specs=placed,
        out_specs=P(None, None, "lat", "lon"),
        check_vma=False,
    )
```

```python
import jax
import jax.numpy as jnp
from jax import lax
from jax.experimental import pallas as pl
from jax.experimental.pallas import tpu as pltpu
from jax.sharding import PartitionSpec as P

F, M, R, C, K = 3, 80, 32, 128, 24
GAIN, INNOV, ALPHA, ROW, COL, KIND = 80, 81, 82, 83, 84, 85
AE, AW, AN, AS, LIST, T = 88, 89, 90, 91, 96, 112
VALUE, ERROR, LIVE = GAIN, INNOV, ALPHA
LATER = 96
S = 80
f32, bf16 = jnp.float32, jnp.bfloat16
VMEM = pltpu.VMEM
MiB = 1 << 20


def lanes(shape):
    return lax.broadcasted_iota(jnp.int32, shape, len(shape) - 1)


def split(x):
    hi = x.astype(bf16)
    return hi, (x - hi.astype(f32)).astype(bf16)


def split3(x):
    hi = x.astype(bf16)
    rest = x - hi.astype(f32)
    mid = rest.astype(bf16)
    return hi, mid, (rest - mid.astype(f32)).astype(bf16)


def dot(a, b, dims=((1,), (0,))):
    return lax.dot_general(a, b, (dims, ((), ())), preferred_element_type=f32)


def subs(shape):
    return lax.broadcasted_iota(jnp.int32, shape, 0)


def parity(axis):
    return lax.rem(lax.axis_index(axis), 2)


def flag(value, shape):
    return (jnp.zeros(shape, jnp.int32) + value) == 1


def stencil(u, v):
    uu, vv = 0.5 * u * u, 0.5 * v * v
    return 1.0 - 2.0 * uu - 2.0 * vv, uu - 0.5 * u, uu + 0.5 * u, vv - 0.5 * v, vv + 0.5 * v


def own_part(b, start, xt, cell, kind, cc, cr, value, error, live, listed, part):
    lane, lane1 = lanes((M, C)), lanes((1, C))
    zero = jnp.zeros((1, C), f32)
    prior = jnp.zeros((M, C), f32)
    rows = [zero] * 7
    for s in range(K):
        at = cell[b, s]
        r, c = at // C, at % C
        f = kind[b, s]
        rf = zero + r.astype(f32)
        here, ae, aw, an, as_ = stencil(cc[0, pl.ds(r, 1), :], cr[0, pl.ds(r, 1), :])
        turn = lax.rem(start + s + C - c, C)
        fields = [rf, zero + c.astype(f32), zero + f.astype(f32)]
        fields += [pltpu.roll(w, turn, 1) for w in (ae, aw, an, as_)]
        mine1 = lane1 == start + s
        rows = [jnp.where(mine1, w, old) for w, old in zip(fields, rows)]
        ae = jnp.where(lane1 == C - 1, 0.0, ae)
        aw = jnp.where(lane1 == 0, 0.0, aw)
        an = jnp.where(rf == R - 1.0, 0.0, an)
        as_ = jnp.where(rf == 0.0, 0.0, as_)
        x = xt[f, r]
        y = here * x + ae * pltpu.roll(x, C - 1, 1) + aw * pltpu.roll(x, 1, 1)
        y = y + an * xt[f, jnp.minimum(r + 1, R - 1)] + as_ * xt[f, jnp.maximum(r - 1, 0)]
        prior = jnp.where(lane == start + s, pltpu.roll(y, turn, 1), prior)
    part[...] = jnp.zeros((T, C), f32)
    part[:M] = prior
    for n, w in zip((ROW, COL, KIND, AE, AW, AN, AS), rows):
        part[n : n + 1, :] = w
    keep = slice(start, start + K)
    part[VALUE : VALUE + 1, keep] = value[b : b + 1, :]
    part[ERROR : ERROR + 1, keep] = error[b : b + 1, :]
    part[LIVE : LIVE + 1, keep] = live[b : b + 1, :].astype(f32)
    for n in range(9):
        part[LIST + n : LIST + n + 1, keep] = listed[n, b : b + 1, :].astype(f32)


def small_copies(srcs, dsts, sems):
    return [pltpu.make_async_copy(a, b, sems.at[n]) for n, (a, b) in enumerate(zip(srcs, dsts))]


def edges_kernel(*refs):
    x_hbm, small = refs[0], refs[1:9]
    xt, pay_a, pay_b = refs[9:12]
    here = refs[12:20]
    buf, acc, sem, small_sem = refs[20:]
    for ib in range(R // 8):
        for f in range(F):
            pltpu.make_async_copy(
                x_hbm.at[f, :, pl.ds(ib * 8, 8), :], buf.at[ib, f], sem.at[ib, f]
            ).start()
    copies = small_copies(small, here, small_sem)
    for c in copies:
        c.start()
    acc[...] = jnp.zeros_like(acc)
    lane = lanes((M, C))
    for ib in range(R // 8):
        for f in range(F):
            pltpu.make_async_copy(
                x_hbm.at[f, :, pl.ds(ib * 8, 8), :], buf.at[ib, f], sem.at[ib, f]
            ).wait()
            rows = buf.at[ib, f].reshape(M * 8, C)
            first, last = acc[0, :M], acc[1, :M]
            for r in range(8):
                v = rows[pl.ds(r, M, stride=8), :]
                i = ib * 8 + r
                k = f * R + i
                xt[f, i] = v
                turned = pltpu.roll(v, k, 1) if k else v
                first = jnp.where(lane == k, turned, first)
                last = jnp.where(lane == (k - 1) % C, turned, last)
            acc[0, :M] = first
            acc[1, :M] = last
    first, last = acc[0, :M], pltpu.roll(acc[1, :M], 1, 1)
    ra = jnp.where(parity("lat") == 1, 0, R - 1)
    rb = R - 1 - ra
    for f in range(F):
        pay_a[pl.ds(f * M, M), :] = xt[f, ra]
        pay_b[pl.ds(f * M, M), :] = xt[f, rb]
    for pay in (pay_a, pay_b):
        pay[pl.ds(F * M, M), :] = first
        pay[pl.ds(F * M + M, M), :] = last
    for c in copies:
        c.wait()
    part = acc.at[2]
    own_part(0, 0, xt, *here, part)
    pay_a[pl.ds(5 * M, T), :] = part[...]
    pay_b[pl.ds(5 * M, T), :] = part[...]


def later_kernel(*refs):
    xt, small, out, here, small_sem = refs[0], refs[1:9], refs[9], refs[10:18], refs[18]
    copies = small_copies(small, here, small_sem)
    for c in copies:
        c.start()
    for c in copies:
        c.wait()
    own_part(1, LATER, xt, *here, out)


def combine(own, a, b):
    few = lanes((T, C)) < K
    return (
        own
        + pltpu.roll(jnp.where(few, a, 0.0), K, 1)
        + pltpu.roll(jnp.where(few, b, 0.0), 2 * K, 1)
    )


def lane_group():
    lane = lanes((1, C))
    group = jnp.where(lane < 2 * K, 1, jnp.where(lane < 3 * K, 2, 3))
    return jnp.where((lane < K) | ((lane >= LATER) & (lane < LATER + K)), 0, group)


def pickup(sources, key):
    hot = (subs((F * C, C)).astype(f32) == key).astype(f32).astype(bf16)
    return sum(dot(h, hot) for h in split3(jnp.concatenate(sources, axis=1)))


def rows_kernel(xt, pay, later, got_a, got_b, out_a, out_b):
    pa, pb = parity("lat"), parity("lon")
    base = 5 * M
    comb = combine(pay[pl.ds(base, T), :], got_a[pl.ds(base, T), :], got_b[pl.ds(base, T), :])
    comb = comb + later[...]
    row, col, kind = comb[ROW : ROW + 1], comb[COL : COL + 1], comb[KIND : KIND + 1]
    group = lane_group()
    edge_a = jnp.where(pa == 1, 0, R - 1)
    edge_b = R - 1 - edge_a
    cellkey = kind * C + col

    def key(n, edge):
        return jnp.where((group == n) & (row == edge.astype(f32)), cellkey, -1.0)

    total = pickup([got_a[pl.ds(f * M, M), :] for f in range(F)], key(0, edge_a))
    total += pickup([got_b[pl.ds(f * M, M), :] for f in range(F)], key(0, edge_b))
    total += pickup([xt[f, edge_a] for f in range(F)], key(1, edge_b))
    total += pickup([xt[f, edge_b] for f in range(F)], key(2, edge_a))
    coef = jnp.where(row == 0.0, comb[AS : AS + 1], comb[AN : AN + 1])
    prior = comb[:M] + coef * total
    odd = flag(pb, (M, C))
    for n, src in enumerate((pay, got_a, got_b)):
        first, last = src[pl.ds(F * M, M), :], src[pl.ds(F * M + M, M), :]
        out_a[pl.ds(n * M, M), :] = jnp.where(odd, first, last)
        out_b[pl.ds(n * M, M), :] = jnp.where(odd, last, first)
    for out in (out_a, out_b):
        out[pl.ds(3 * M, M), :] = prior
        out[pl.ds(4 * M, T - M), :] = comb[M:]


def statistics(t):
    prior = t[:M]
    ybar = jnp.sum(prior, axis=0, keepdims=True) / M
    yp = prior - ybar
    spread = jnp.sum(yp * yp, axis=0, keepdims=True) / (M - 1)
    err = t[ERROR : ERROR + 1]
    total = spread + err
    total = jnp.where(total == 0.0, 1.0, total)
    gain = t[LIVE : LIVE + 1] / total
    alpha = 1.0 / (1.0 + jnp.sqrt(err / total))
    innov = t[VALUE : VALUE + 1] - ybar
    return yp, gain, innov, alpha


def stack_fields(yp, rows):
    sub = subs((16, C))
    extra = jnp.zeros((16, C), f32)
    for n, v in enumerate(rows):
        extra = jnp.where(sub == n, v, extra)
    return jnp.concatenate([yp, extra], axis=0)


def choose(index, raw, yp, gain, innov, alpha):
    sa = 1 - 2 * parity("lat")
    sb = 1 - 2 * parity("lon")
    db = (0, sb, -sb)[index]
    group = lane_group()
    chosen = jnp.zeros((1, C), f32)
    row = raw[ROW : ROW + 1, :]
    for n, da in enumerate((0, sa, -sa)):
        listed = raw[pl.ds(LIST + (1 - da) * 3 + (1 - db), 1), :]
        chosen = jnp.where(group == n, listed, chosen)
        row = jnp.where(group == n, row + jnp.asarray(da * R, f32), row)
    col = raw[COL : COL + 1, :] + jnp.asarray(db * C, f32)
    factor = gain * chosen
    near = (row > -float(R)) & (row < 2.0 * R - 1.0) & (col > -float(R)) & (col < C + R - 1.0)
    act = near & (factor != 0.0) & (lanes((1, C)) < 3 * K)
    return stack_fields(yp, (factor, innov, alpha, row, col)), jnp.where(act, 1.0, 0.0)


def ranks(actives):
    before = (subs((C, C)) < lanes((C, C))).astype(f32).astype(bf16)
    out, offset = [], jnp.zeros((1, 1), f32)
    for act in actives:
        r = dot(jnp.broadcast_to(act, (8, C)).astype(bf16), before)[:1] + offset
        out.append(jnp.where(act > 0.0, r, -1.0))
        offset = offset + jnp.sum(act, axis=1, keepdims=True)
    return out, sum(jnp.sum(a) for a in actives).astype(jnp.int32)


def spread_lanes(hi, lo):
    r = lax.broadcasted_iota(jnp.int32, (C, 2 * C), 0)
    c = lax.broadcasted_iota(jnp.int32, (C, 2 * C), 1)
    keep = r < S
    e_hi = (((c == r) | (c == r + 2 * S)) & keep).astype(f32).astype(bf16)
    e_lo = ((c == r + S) & keep).astype(f32).astype(bf16)
    return (dot(hi, e_hi) + dot(lo, e_lo)).astype(bf16)


def compact(fields, rank, chunk, ycat, bcat, locs):
    p = subs((C, F * C)).astype(f32) + jnp.asarray(chunk * S, f32)
    own = subs((C, F * C)) < S
    pick = ((rank == p) & own).astype(f32).astype(bf16)
    turned = sum(dot(t, pick, ((1,), (1,))) for t in split3(fields))
    chosen = jnp.concatenate([turned, jnp.zeros((32, C), f32)], axis=0).T[:S]
    ycat[chunk] = spread_lanes(*split(chosen))
    back = turned[INNOV : INNOV + 1, :] - turned[ALPHA : ALPHA + 1, :] * turned[:M]
    bcat[chunk] = spread_lanes(*split(back))
    locs[chunk, 0] = jnp.broadcast_to(chosen[:, ROW : ROW + 1], (S, C))
    locs[chunk, 1] = jnp.broadcast_to(chosen[:, COL : COL + 1], (S, C))
    locs[chunk, 2] = jnp.broadcast_to(chosen[:, GAIN : GAIN + 1], (S, C)) / (M - 1)


def compact_all(fields, rank, count, ycat, bcat, locs):
    compact(fields, rank, 0, ycat, bcat, locs)

    @pl.when(count > S)
    def _():
        def body(j, carry):
            compact(fields, rank, j, ycat, bcat, locs)
            return carry

        lax.fori_loop(1, (count + S - 1) // S, body, 0)


def taper(d):
    z = jnp.maximum(0.0, 1.0 - jnp.abs(d) / R)
    return z * z


def update(p, lw, ycat, bcat):
    hi, lo = split(p)
    none = jnp.zeros((2 * C - 3 * M, p.shape[1]), bf16)
    proj = dot(ycat, jnp.concatenate([hi, hi, lo, none], axis=0))
    hi, lo = split(proj * lw)
    return dot(bcat, jnp.concatenate([hi, hi, lo, none], axis=0))


def tables_kernel(pay, got_a, got_b, own_in, got_x, got_y, after, table, count_out, ycat, bcat, locs):
    pb = parity("lon")
    edge_x = jnp.where(pb == 1, 0.0, C - 1.0)
    edge_y = C - 1.0 - edge_x
    group = lane_group()
    odd = flag(pb, (M, C))
    mine_x, mine_y = [], []
    for src in (pay, got_a, got_b):
        first, last = src[pl.ds(F * M, M), :], src[pl.ds(F * M + M, M), :]
        mine_x.append(jnp.where(odd, first, last))
        mine_y.append(jnp.where(odd, last, first))

    def complete(t, parts):
        row, col, kind = t[ROW : ROW + 1], t[COL : COL + 1], t[KIND : KIND + 1]
        at = group.astype(f32) * C + kind * R + row
        total = jnp.zeros((M, C), f32)
        for packs, edge in parts:
            total += pickup(packs, jnp.where((group < 3) & (col == edge), at, -1.0))
        coef = jnp.where(col == 0.0, t[AW : AW + 1], t[AE : AE + 1])
        return t[:M] + coef * total

    def packs(got):
        return [got[pl.ds(n * M, M), :] for n in range(3)]

    base = 3 * M
    out = []
    later = None
    for index, (src, parts) in enumerate((
        (own_in, ((packs(got_x), edge_x), (packs(got_y), edge_y))),
        (got_x, ((mine_x, edge_y),)),
        (got_y, ((mine_y, edge_x),)),
    )):
        raw = src.at[pl.ds(base, T), :]
        t = raw[...]
        whole = jnp.concatenate([complete(t, parts), t[M:]], axis=0)
        if index == 0:
            later = whole
        out.append(choose(index, raw, *statistics(whole)))
    fields = jnp.concatenate([a for a, _ in out], axis=1)
    rank, count = ranks([a for _, a in out])
    rank = jnp.concatenate(rank, axis=1)
    count_out[0] = count
    compact_all(fields, rank, count, ycat, bcat, locs)

    prior = later[:M]
    row, col = later[ROW : ROW + 1], later[COL : COL + 1]

    def point(j, add):
        lw = taper(locs[j, 0] - row) * taper(locs[j, 1] - col) * locs[j, 2]
        return add + update(prior, lw, ycat[j], bcat[j])

    add = lax.fori_loop(0, jnp.maximum((count + S - 1) // S, 1), point, jnp.zeros((M, C), f32))
    later = jnp.concatenate([prior + add, later[M:]], axis=0)
    yp, gain, innov, alpha = statistics(later)
    fresh = stack_fields(yp, (gain, innov, alpha, row, col))
    fresh = jnp.concatenate([fresh, later[LIST:]], axis=0)
    lane = lanes((T, C))
    fresh = jnp.where((lane >= LATER) & (lane < LATER + K), fresh, 0.0)
    table[...] = pltpu.roll(fresh, C - LATER, 1)


def combine_kernel(own, a, b, out):
    out[...] = combine(own[...], a[...], b[...])


def advect_kernel(xt, got_a, got_b, cc_hbm, cr_hbm, state, edge, cc, cr, sems):
    copies = small_copies((cc_hbm, cr_hbm), (cc, cr), sems)
    for c in copies:
        c.start()
    for c in copies:
        c.wait()
    lane1 = lanes((1, C))
    odd_a = flag(parity("lat"), (M, C))

    def one(i, low, high):
        here, ae, aw, an, as_ = stencil(cc[0, pl.ds(i, 1), :], cr[0, pl.ds(i, 1), :])
        edge[pl.ds(i, 1), :] = jnp.where(
            lane1 == 0, aw, jnp.where(lane1 == C - 1, ae, 0.0)
        )
        ae = jnp.where(lane1 == C - 1, 0.0, ae)
        aw = jnp.where(lane1 == 0, 0.0, aw)
        for f in range(F):
            x = xt[f, i]
            ha, hb = got_a[pl.ds(f * M, M), :], got_b[pl.ds(f * M, M), :]
            xs = jnp.where(odd_a, ha, hb) if low else xt[f, i - 1]
            xn = jnp.where(odd_a, hb, ha) if high else xt[f, i + 1]
            y = here * x + ae * pltpu.roll(x, C - 1, 1) + aw * pltpu.roll(x, 1, 1)
            state[f, i] = y + an * xn + as_ * xs

    one(0, True, False)
    one(R - 1, False, True)

    def body(n, carry):
        one(2 * n + 1, False, False)
        one(2 * n + 2, False, False)
        return carry

    lax.fori_loop(0, R // 2 - 1, body, 0)


def lay_halos(got_x, got_y, merged):
    odd_lane = (lanes((M, C)) % 2) == 1
    odd_b = flag(parity("lon"), (M, C))
    got_1, got_2 = got_x[pl.ds(0, M), :], got_y[pl.ds(0, M), :]
    east = pltpu.roll(jnp.where(odd_b, got_2, got_1), C - 1, 1)
    west = jnp.where(odd_b, got_1, got_2)
    merged[0] = jnp.where(odd_lane, east, west)
    merged[1] = jnp.where(odd_lane, west, east)


def sweeps(row_of, count, ycat, bcat, locs, col_w, total, emit):
    def weigh(j):
        col_w[...] = taper(locs[j, 1] - lanes((S, C)).astype(f32)) * locs[j, 2]

    def sweep(base, j, put):
        def local(i):
            return taper(locs[j, 0] - i.astype(f32)) * col_w[...]

        def body(n, carry):
            i = 2 * n
            lw = jnp.concatenate([local(i), local(i + 1)], axis=1)
            for f in range(F):
                pair = row_of(f, i, 0), row_of(f, i + 1, 1)
                d = update(jnp.concatenate(pair, axis=1), lw, ycat[j], bcat[j])
                if base is not None:
                    pair = base[f, i], base[f, i + 1]
                put(n, f, pair[0] + d[:, :C], pair[1] + d[:, C:])
            return carry

        return body

    def keep(n, f, a, b):
        total[f, 2 * n] = a
        total[f, 2 * n + 1] = b

    @pl.when(count > S)
    def _():
        weigh(1)
        lax.fori_loop(0, R // 2, sweep(None, 1, keep), 0)

        @pl.when(count > 2 * S)
        def _():
            weigh(2)
            lax.fori_loop(0, R // 2, sweep(total, 2, keep), 0)

        weigh(0)
        emit(sweep, total)

    @pl.when(count <= S)
    def _():
        weigh(0)
        emit(sweep, None)


def first_kernel(count, state, edge, got_x, got_y, ycat, bcat, locs, out, col_w, total, merged):
    lay_halos(got_x, got_y, merged)

    def row_of(f, i, odd):
        halo = pltpu.roll(merged[odd], lax.rem(2 * C - (f * R + i), C), 1)
        return state[f, i] + halo * edge[pl.ds(i, 1), :]

    def emit(sweep, base):
        def put(n, f, a, b):
            out[f, 2 * n] = a
            out[f, 2 * n + 1] = b

        lax.fori_loop(0, R // 2, sweep(base, 0, put), 0)

    sweeps(row_of, count[0], ycat, bcat, locs, col_w, total, emit)


def second_kernel(own, got_x, got_y, state, out, buf, sem, ycat, bcat, locs, col_w, total):
    parts = []
    for index, raw in enumerate((own, got_x, got_y)):
        t = raw[...]
        rows = (t[GAIN : GAIN + 1], t[INNOV : INNOV + 1], t[ALPHA : ALPHA + 1])
        parts.append(choose(index, raw, t[:M], *rows))
    rank, count = ranks([a for _, a in parts])
    fields = jnp.concatenate([a for a, _ in parts], axis=1)
    compact_all(fields, jnp.concatenate(rank, axis=1), count, ycat, bcat, locs)

    def copy(ib, f):
        return pltpu.make_async_copy(
            buf.at[ib, f], out.at[f, :, pl.ds(ib * 8, 8), :], sem.at[ib, f]
        )

    def emit(sweep, base):
        for ib in range(R // 8):

            def put(n, f, a, b):
                rows = buf.at[ib, f].reshape(M * 8, C)
                r = 2 * (n - 4 * ib)
                rows[pl.ds(r, M, stride=8), :] = a
                rows[pl.ds(r + 1, M, stride=8), :] = b

            lax.fori_loop(4 * ib, 4 * ib + 4, sweep(base, 0, put), 0)
            for f in range(F):
                copy(ib, f).start()

    sweeps(lambda f, i, odd: state[f, i], count, ycat, bcat, locs, col_w, total, emit)
    for ib in range(R // 8):
        for f in range(F):
            copy(ib, f).wait()


def call(kernel, outs, args, scratch=(), scalars=0, hbm=(), out_spaces=None, us=2, limit=24):
    spaces = [
        pltpu.SMEM if n < scalars else pltpu.HBM if n in hbm else VMEM for n in range(len(args))
    ]
    args = [
        pltpu.with_memory_space_constraint(a, s) if a.size > 100000 or s == pltpu.HBM else a
        for a, s in zip(args, spaces)
    ]
    out_spaces = out_spaces or [VMEM] * len(outs)
    return pl.pallas_call(
        kernel,
        out_shape=outs,
        in_specs=[pl.BlockSpec(memory_space=s) for s in spaces],
        out_specs=[pl.BlockSpec(memory_space=s) for s in out_spaces],
        scratch_shapes=scratch,
        compiler_params=pltpu.CompilerParams(vmem_limit_bytes=limit * MiB),
        cost_estimate=pl.CostEstimate(flops=0, transcendentals=0, bytes_accessed=us * 3000000),
        name=kernel.__name__,
    )(*args)


def swap(x, axis, shift):
    n = lax.axis_size(axis)
    pairs = [(i, ((i - shift) ^ 1) + shift) for i in range(n)]
    pairs = [(i, j) for i, j in pairs if i >= shift and 0 <= j < n]
    return lax.ppermute(x, axis, pairs)


def on_device(
    ensemble, courant_cols, courant_rows, obs_value, obs_error, obs_cell, obs_kind, obs_live, obs_list
):
    listed = jnp.transpose(obs_list, (2, 0, 1))
    block = VMEM((F, R, M, C), f32)
    sds = jax.ShapeDtypeStruct
    copies = [VMEM((R // 8, F, M, 8, C), f32)]
    sems = pltpu.SemaphoreType.DMA((R // 8, F))

    small = [
        obs_cell, obs_kind, courant_cols, courant_rows, obs_value, obs_error, obs_live, listed
    ]
    held = [(pltpu.SMEM if n < 2 else VMEM)(a.shape, a.dtype) for n, a in enumerate(small)]
    held_sems = pltpu.SemaphoreType.DMA((len(small),))

    pay_shape = sds((5 * M + T, C), f32)
    xt, pay_a, pay_b = call(
        edges_kernel,
        [block, pay_shape, pay_shape],
        [ensemble, *small],
        [*held, *copies, VMEM((3, T, C), f32), sems, held_sems],
        hbm=range(9),
    )
    got_b, got_a = swap(pay_b, "lat", 1), swap(pay_a, "lat", 0)
    later = call(
        later_kernel, [sds((T, C), f32)], [xt, *small], [*held, held_sems], hbm=range(1, 9), us=1
    )[0]
    lon_shape = sds((3 * M + T, C), f32)
    out_a, out_b = call(rows_kernel, [lon_shape] * 2, [xt, pay_a, later, got_a, got_b])
    got_y, got_x = swap(out_b, "lon", 1), swap(out_a, "lon", 0)
    state, edge = call(
        advect_kernel,
        [block, sds((R, C), f32)],
        [xt, got_a, got_b, courant_cols, courant_rows],
        [held[2], held[3], pltpu.SemaphoreType.DMA((2,))],
        hbm=(3, 4),
    )
    chosen = [sds((3, S, 2 * C), bf16), sds((3, M, 2 * C), bf16), sds((3, 3, S, C), f32)]
    table, count, *picked = call(
        tables_kernel,
        [sds((T, C), f32), sds((1,), jnp.int32), *chosen],
        [pay_a, got_a, got_b, out_a, got_x, got_y, edge],
        out_spaces=[VMEM, pltpu.SMEM, VMEM, VMEM, VMEM],
    )
    tab_b, tab_a = swap(table, "lat", 1), swap(table, "lat", 0)
    column = call(combine_kernel, [sds((T, C), f32)], [table, tab_a, tab_b], us=1)[0]
    col_y, col_x = swap(column, "lon", 1), swap(column, "lon", 0)
    work = [VMEM((S, C), f32), VMEM((F, R, M, C), f32)]
    state = call(
        first_kernel,
        [block],
        [count, state, edge, got_x, got_y, *picked],
        work + [VMEM((2, M, C), f32)],
        scalars=1,
        us=4,
    )[0]
    return call(
        second_kernel,
        [sds((F, M, R, C), f32)],
        [column, col_x, col_y, state],
        [*copies, sems]
        + [VMEM((3, S, 2 * C), bf16), VMEM((3, M, 2 * C), bf16), VMEM((3, 3, S, C), f32)]
        + work,
        out_spaces=[pltpu.HBM],
        us=6,
    )[0]


def solution(mesh):
    tiles = P(None, ("lat", "lon"))
    placed = (
        P(None, None, "lat", "lon"),
        P(None, "lat", "lon"),
        P(None, "lat", "lon"),
        tiles,
        tiles,
        tiles,
        tiles,
        tiles,
        P(None, ("lat", "lon"), None),
    )
    return jax.shard_map(
        on_device,
        mesh=mesh,
        in_specs=placed,
        out_specs=P(None, None, "lat", "lon"),
        check_vma=False,
    )
```

```python
import jax
import jax.numpy as jnp
from jax import lax
from jax.experimental import pallas as pl
from jax.experimental.pallas import tpu as pltpu
from jax.sharding import PartitionSpec as P

F, M, R, C, K = 3, 80, 32, 128, 24
GAIN, INNOV, ALPHA, ROW, COL, KIND = 80, 81, 82, 83, 84, 85
AE, AW, AN, AS, LIST, T = 88, 89, 90, 91, 96, 112
VALUE, ERROR, LIVE = GAIN, INNOV, ALPHA
LATER = 96
S = 80
STEP = 4
f32, bf16 = jnp.float32, jnp.bfloat16
VMEM = pltpu.VMEM
MiB = 1 << 20


def lanes(shape):
    return lax.broadcasted_iota(jnp.int32, shape, len(shape) - 1)


def split(x):
    hi = x.astype(bf16)
    return hi, (x - hi.astype(f32)).astype(bf16)


def split3(x):
    hi = x.astype(bf16)
    rest = x - hi.astype(f32)
    mid = rest.astype(bf16)
    return hi, mid, (rest - mid.astype(f32)).astype(bf16)


def dot(a, b, dims=((1,), (0,))):
    return lax.dot_general(a, b, (dims, ((), ())), preferred_element_type=f32)


def subs(shape):
    return lax.broadcasted_iota(jnp.int32, shape, 0)


def parity(axis):
    return lax.rem(lax.axis_index(axis), 2)


def flag(value, shape):
    return (jnp.zeros(shape, jnp.int32) + value) == 1


def stencil(u, v):
    uu, vv = 0.5 * u * u, 0.5 * v * v
    return 1.0 - 2.0 * uu - 2.0 * vv, uu - 0.5 * u, uu + 0.5 * u, vv - 0.5 * v, vv + 0.5 * v


def own_part(b, start, xt, cell, kind, cc, cr, value, error, live, listed, part):
    lane, lane1, lane8 = lanes((M, C)), lanes((1, C)), lanes((8, C))
    sub8 = subs((8, C))
    zero = jnp.zeros((1, C), f32)
    prior = jnp.zeros((M, C), f32)
    coefs = jnp.zeros((8, C), f32)
    rows = [zero] * 3
    for s in range(K):
        at = cell[b, s]
        r, c = lax.shift_right_logical(at, 7), lax.bitwise_and(at, C - 1)
        f = kind[b, s]
        rf = zero + r.astype(f32)
        mine1 = lane1 == start + s
        fields = (rf, zero + c.astype(f32), zero + f.astype(f32))
        rows = [jnp.where(mine1, w, old) for w, old in zip(fields, rows)]
        here, ae, aw, an, as_ = (
            jnp.where(lane1 == c, w, 0.0)
            for w in stencil(cc[0, pl.ds(r, 1), :], cr[0, pl.ds(r, 1), :])
        )
        stack = jnp.where(
            sub8 == 0, ae, jnp.where(sub8 == 1, aw, jnp.where(sub8 == 2, an, as_))
        )
        total = jnp.sum(stack, axis=1, keepdims=True)
        coefs = jnp.where(lane8 == start + s, total, coefs)
        ae = pltpu.roll(jnp.where(lane1 == C - 1, 0.0, ae), 1, 1)
        aw = pltpu.roll(jnp.where(lane1 == 0, 0.0, aw), C - 1, 1)
        an = jnp.where(rf == R - 1.0, 0.0, an)
        as_ = jnp.where(rf == 0.0, 0.0, as_)
        y = (here + ae + aw) * xt[f, r]
        y = y + an * xt[f, jnp.minimum(r + 1, R - 1)] + as_ * xt[f, jnp.maximum(r - 1, 0)]
        prior = jnp.where(lane == start + s, jnp.sum(y, axis=1, keepdims=True), prior)
    part[...] = jnp.zeros((T, C), f32)
    part[:M] = prior
    for n, w in zip((ROW, COL, KIND), rows):
        part[n : n + 1, :] = w
    part[AE : AE + 8, :] = coefs
    keep = slice(start, start + K)
    part[VALUE : VALUE + 1, keep] = value[b : b + 1, :]
    part[ERROR : ERROR + 1, keep] = error[b : b + 1, :]
    part[LIVE : LIVE + 1, keep] = live[b : b + 1, :].astype(f32)
    for n in range(9):
        part[LIST + n : LIST + n + 1, keep] = listed[n, b : b + 1, :].astype(f32)


def small_copies(srcs, dsts, sems):
    return [pltpu.make_async_copy(a, b, sems.at[n]) for n, (a, b) in enumerate(zip(srcs, dsts))]


def edges_kernel(*refs):
    x_hbm, small = refs[0], refs[1:9]
    xt, pay_a, pay_b = refs[9:12]
    here = refs[12:20]
    buf, acc, sem, small_sem = refs[20:]
    for ib in range(R // 8):
        for f in range(F):
            pltpu.make_async_copy(
                x_hbm.at[f, :, pl.ds(ib * 8, 8), :], buf.at[ib, f], sem.at[ib, f]
            ).start()
    copies = small_copies(small, here, small_sem)
    for c in copies:
        c.start()
    acc[...] = jnp.zeros_like(acc)
    lane = lanes((M, C))
    for ib in range(R // 8):
        for f in range(F):
            pltpu.make_async_copy(
                x_hbm.at[f, :, pl.ds(ib * 8, 8), :], buf.at[ib, f], sem.at[ib, f]
            ).wait()
            rows = buf.at[ib, f].reshape(M * 8, C)
            first, last = acc[0, :M], acc[1, :M]
            for r in range(8):
                v = rows[pl.ds(r, M, stride=8), :]
                i = ib * 8 + r
                k = f * R + i
                xt[f, i] = v
                turned = pltpu.roll(v, k, 1) if k else v
                first = jnp.where(lane == k, turned, first)
                last = jnp.where(lane == (k - 1) % C, turned, last)
            acc[0, :M] = first
            acc[1, :M] = last
    first, last = acc[0, :M], pltpu.roll(acc[1, :M], 1, 1)
    ra = jnp.where(parity("lat") == 1, 0, R - 1)
    rb = R - 1 - ra
    for f in range(F):
        pay_a[pl.ds(f * M, M), :] = xt[f, ra]
        pay_b[pl.ds(f * M, M), :] = xt[f, rb]
    for pay in (pay_a, pay_b):
        pay[pl.ds(F * M, M), :] = first
        pay[pl.ds(F * M + M, M), :] = last
    for c in copies:
        c.wait()
    part = acc.at[2]
    own_part(0, 0, xt, *here, part)
    pay_a[pl.ds(5 * M, T), :] = part[...]
    pay_b[pl.ds(5 * M, T), :] = part[...]


def later_kernel(*refs):
    xt, small, out, here, small_sem = refs[0], refs[1:9], refs[9], refs[10:18], refs[18]
    copies = small_copies(small, here, small_sem)
    for c in copies:
        c.start()
    for c in copies:
        c.wait()
    own_part(1, LATER, xt, *here, out)


def combine(own, a, b):
    few = lanes((T, C)) < K
    return (
        own
        + pltpu.roll(jnp.where(few, a, 0.0), K, 1)
        + pltpu.roll(jnp.where(few, b, 0.0), 2 * K, 1)
    )


def lane_group():
    lane = lanes((1, C))
    group = jnp.where(lane < 2 * K, 1, jnp.where(lane < 3 * K, 2, 3))
    return jnp.where((lane < K) | ((lane >= LATER) & (lane < LATER + K)), 0, group)


def pickup(sources, key):
    hot = (subs((F * C, C)).astype(f32) == key).astype(f32).astype(bf16)
    return sum(dot(h, hot) for h in split3(jnp.concatenate(sources, axis=1)))


def rows_kernel(xt, pay, later, got_a, got_b, out_a, out_b):
    pa, pb = parity("lat"), parity("lon")
    base = 5 * M
    comb = combine(pay[pl.ds(base, T), :], got_a[pl.ds(base, T), :], got_b[pl.ds(base, T), :])
    comb = comb + later[...]
    row, col, kind = comb[ROW : ROW + 1], comb[COL : COL + 1], comb[KIND : KIND + 1]
    group = lane_group()
    edge_a = jnp.where(pa == 1, 0, R - 1)
    edge_b = R - 1 - edge_a
    cellkey = kind * C + col

    def key(n, edge):
        return jnp.where((group == n) & (row == edge.astype(f32)), cellkey, -1.0)

    total = pickup([got_a[pl.ds(f * M, M), :] for f in range(F)], key(0, edge_a))
    total += pickup([got_b[pl.ds(f * M, M), :] for f in range(F)], key(0, edge_b))
    total += pickup([xt[f, edge_a] for f in range(F)], key(1, edge_b))
    total += pickup([xt[f, edge_b] for f in range(F)], key(2, edge_a))
    coef = jnp.where(row == 0.0, comb[AS : AS + 1], comb[AN : AN + 1])
    prior = comb[:M] + coef * total
    odd = flag(pb, (M, C))
    for n, src in enumerate((pay, got_a, got_b)):
        first, last = src[pl.ds(F * M, M), :], src[pl.ds(F * M + M, M), :]
        out_a[pl.ds(n * M, M), :] = jnp.where(odd, first, last)
        out_b[pl.ds(n * M, M), :] = jnp.where(odd, last, first)
    for out in (out_a, out_b):
        out[pl.ds(3 * M, M), :] = prior
        out[pl.ds(4 * M, T - M), :] = comb[M:]


def statistics(t):
    prior = t[:M]
    ybar = jnp.sum(prior, axis=0, keepdims=True) / M
    yp = prior - ybar
    spread = jnp.sum(yp * yp, axis=0, keepdims=True) / (M - 1)
    err = t[ERROR : ERROR + 1]
    total = spread + err
    total = jnp.where(total == 0.0, 1.0, total)
    gain = t[LIVE : LIVE + 1] / total
    alpha = 1.0 / (1.0 + jnp.sqrt(err / total))
    innov = t[VALUE : VALUE + 1] - ybar
    return yp, gain, innov, alpha


def stack_fields(yp, rows):
    sub = subs((16, C))
    extra = jnp.zeros((16, C), f32)
    for n, v in enumerate(rows):
        extra = jnp.where(sub == n, v, extra)
    return jnp.concatenate([yp, extra], axis=0)


def choose(index, raw, yp, gain, innov, alpha):
    sa = 1 - 2 * parity("lat")
    sb = 1 - 2 * parity("lon")
    db = (0, sb, -sb)[index]
    group = lane_group()
    chosen = jnp.zeros((1, C), f32)
    row = raw[ROW : ROW + 1, :]
    for n, da in enumerate((0, sa, -sa)):
        listed = raw[pl.ds(LIST + (1 - da) * 3 + (1 - db), 1), :]
        chosen = jnp.where(group == n, listed, chosen)
        row = jnp.where(group == n, row + jnp.asarray(da * R, f32), row)
    col = raw[COL : COL + 1, :] + jnp.asarray(db * C, f32)
    factor = gain * chosen
    near = (row > -float(R)) & (row < 2.0 * R - 1.0) & (col > -float(R)) & (col < C + R - 1.0)
    act = near & (factor != 0.0) & (lanes((1, C)) < 3 * K)
    return stack_fields(yp, (factor, innov, alpha, row, col)), jnp.where(act, 1.0, 0.0)


def ranks(actives):
    before = (subs((C, C)) < lanes((C, C))).astype(f32).astype(bf16)
    out, offset = [], jnp.zeros((1, 1), f32)
    for act in actives:
        r = dot(jnp.broadcast_to(act, (8, C)).astype(bf16), before)[:1] + offset
        out.append(jnp.where(act > 0.0, r, -1.0))
        offset = offset + jnp.sum(act, axis=1, keepdims=True)
    return out, sum(jnp.sum(a) for a in actives).astype(jnp.int32)


def spread_lanes(hi, lo):
    r = lax.broadcasted_iota(jnp.int32, (C, 2 * C), 0)
    c = lax.broadcasted_iota(jnp.int32, (C, 2 * C), 1)
    keep = r < S
    e_hi = (((c == r) | (c == r + 2 * S)) & keep).astype(f32).astype(bf16)
    e_lo = ((c == r + S) & keep).astype(f32).astype(bf16)
    return (dot(hi, e_hi) + dot(lo, e_lo)).astype(bf16)


def compact(fields, rank, chunk, ycat, bcat, locs):
    p = subs((C, F * C)).astype(f32) + jnp.asarray(chunk * S, f32)
    own = subs((C, F * C)) < S
    pick = ((rank == p) & own).astype(f32).astype(bf16)
    turned = sum(dot(t, pick, ((1,), (1,))) for t in split3(fields))
    chosen = jnp.concatenate([turned, jnp.zeros((32, C), f32)], axis=0).T[:S]
    ycat[chunk] = spread_lanes(*split(chosen))
    back = turned[INNOV : INNOV + 1, :] - turned[ALPHA : ALPHA + 1, :] * turned[:M]
    bcat[chunk] = spread_lanes(*split(back))
    locs[chunk, 0] = jnp.broadcast_to(chosen[:, ROW : ROW + 1], (S, C))
    locs[chunk, 1] = jnp.broadcast_to(chosen[:, COL : COL + 1], (S, C))
    locs[chunk, 2] = jnp.broadcast_to(chosen[:, GAIN : GAIN + 1], (S, C)) / (M - 1)


def compact_all(fields, rank, count, ycat, bcat, locs):
    compact(fields, rank, 0, ycat, bcat, locs)

    @pl.when(count > S)
    def _():
        def body(j, carry):
            compact(fields, rank, j, ycat, bcat, locs)
            return carry

        lax.fori_loop(1, (count + S - 1) // S, body, 0)


def taper(d):
    z = jnp.maximum(0.0, 1.0 - jnp.abs(d) / R)
    return z * z


def update(p, lw, ycat, bcat):
    hi, lo = split(p)
    none = jnp.zeros((2 * C - 3 * M, p.shape[1]), bf16)
    proj = dot(ycat, jnp.concatenate([hi, hi, lo, none], axis=0))
    hi, lo = split(proj * lw)
    return dot(bcat, jnp.concatenate([hi, hi, lo, none], axis=0))


def tables_kernel(pay, got_a, got_b, own_in, got_x, got_y, after, table, count_out, ycat, bcat, locs):
    pb = parity("lon")
    edge_x = jnp.where(pb == 1, 0.0, C - 1.0)
    edge_y = C - 1.0 - edge_x
    group = lane_group()
    odd = flag(pb, (M, C))
    mine_x, mine_y = [], []
    for src in (pay, got_a, got_b):
        first, last = src[pl.ds(F * M, M), :], src[pl.ds(F * M + M, M), :]
        mine_x.append(jnp.where(odd, first, last))
        mine_y.append(jnp.where(odd, last, first))

    def complete(t, parts):
        row, col, kind = t[ROW : ROW + 1], t[COL : COL + 1], t[KIND : KIND + 1]
        at = group.astype(f32) * C + kind * R + row
        total = jnp.zeros((M, C), f32)
        for packs, edge in parts:
            total += pickup(packs, jnp.where((group < 3) & (col == edge), at, -1.0))
        coef = jnp.where(col == 0.0, t[AW : AW + 1], t[AE : AE + 1])
        return t[:M] + coef * total

    def packs(got):
        return [got[pl.ds(n * M, M), :] for n in range(3)]

    base = 3 * M
    out = []
    later = None
    for index, (src, parts) in enumerate((
        (own_in, ((packs(got_x), edge_x), (packs(got_y), edge_y))),
        (got_x, ((mine_x, edge_y),)),
        (got_y, ((mine_y, edge_x),)),
    )):
        raw = src.at[pl.ds(base, T), :]
        t = raw[...]
        whole = jnp.concatenate([complete(t, parts), t[M:]], axis=0)
        if index == 0:
            later = whole
        out.append(choose(index, raw, *statistics(whole)))
    fields = jnp.concatenate([a for a, _ in out], axis=1)
    rank, count = ranks([a for _, a in out])
    rank = jnp.concatenate(rank, axis=1)
    count_out[0] = count
    compact_all(fields, rank, count, ycat, bcat, locs)

    prior = later[:M]
    row, col = later[ROW : ROW + 1], later[COL : COL + 1]

    def point(j, add):
        lw = taper(locs[j, 0] - row) * taper(locs[j, 1] - col) * locs[j, 2]
        return add + update(prior, lw, ycat[j], bcat[j])

    add = lax.fori_loop(0, jnp.maximum((count + S - 1) // S, 1), point, jnp.zeros((M, C), f32))
    later = jnp.concatenate([prior + add, later[M:]], axis=0)
    yp, gain, innov, alpha = statistics(later)
    fresh = stack_fields(yp, (gain, innov, alpha, row, col))
    fresh = jnp.concatenate([fresh, later[LIST:]], axis=0)
    lane = lanes((T, C))
    fresh = jnp.where((lane >= LATER) & (lane < LATER + K), fresh, 0.0)
    table[...] = pltpu.roll(fresh, C - LATER, 1)


def combine_kernel(own, a, b, out):
    out[...] = combine(own[...], a[...], b[...])


def advect_kernel(xt, got_a, got_b, cc_hbm, cr_hbm, state, edge, cc, cr, sems):
    copies = small_copies((cc_hbm, cr_hbm), (cc, cr), sems)
    for c in copies:
        c.start()
    for c in copies:
        c.wait()
    lane1 = lanes((1, C))
    odd_a = flag(parity("lat"), (M, C))

    def one(i, low, high):
        here, ae, aw, an, as_ = stencil(cc[0, pl.ds(i, 1), :], cr[0, pl.ds(i, 1), :])
        edge[pl.ds(i, 1), :] = jnp.where(
            lane1 == 0, aw, jnp.where(lane1 == C - 1, ae, 0.0)
        )
        ae = jnp.where(lane1 == C - 1, 0.0, ae)
        aw = jnp.where(lane1 == 0, 0.0, aw)
        for f in range(F):
            x = xt[f, i]
            ha, hb = got_a[pl.ds(f * M, M), :], got_b[pl.ds(f * M, M), :]
            xs = jnp.where(odd_a, ha, hb) if low else xt[f, i - 1]
            xn = jnp.where(odd_a, hb, ha) if high else xt[f, i + 1]
            y = here * x + ae * pltpu.roll(x, C - 1, 1) + aw * pltpu.roll(x, 1, 1)
            state[f, i] = y + an * xn + as_ * xs

    one(0, True, False)
    one(R - 1, False, True)

    def body(n, carry):
        one(2 * n + 1, False, False)
        one(2 * n + 2, False, False)
        return carry

    lax.fori_loop(0, R // 2 - 1, body, 0)


def lay_halos(got_x, got_y, merged):
    odd_lane = (lanes((M, C)) % 2) == 1
    odd_b = flag(parity("lon"), (M, C))
    got_1, got_2 = got_x[pl.ds(0, M), :], got_y[pl.ds(0, M), :]
    east = pltpu.roll(jnp.where(odd_b, got_2, got_1), C - 1, 1)
    west = jnp.where(odd_b, got_1, got_2)
    merged[0] = jnp.where(odd_lane, east, west)
    merged[1] = jnp.where(odd_lane, west, east)


def sweeps(row_of, count, ycat, bcat, locs, col_w, total, emit):
    def weigh(j):
        col_w[...] = taper(locs[j, 1] - lanes((S, C)).astype(f32)) * locs[j, 2]

    def sweep(base, j, put):
        def local(i):
            return taper(locs[j, 0] - i.astype(f32)) * col_w[...]

        def body(step, carry):
            for n in [step * STEP + u for u in range(STEP)]:
                i = 2 * n
                lw = jnp.concatenate([local(i), local(i + 1)], axis=1)
                for f in range(F):
                    pair = row_of(f, i, 0), row_of(f, i + 1, 1)
                    d = update(jnp.concatenate(pair, axis=1), lw, ycat[j], bcat[j])
                    if base is not None:
                        pair = base[f, i], base[f, i + 1]
                    put(n, f, pair[0] + d[:, :C], pair[1] + d[:, C:])
            return carry

        return body

    def keep(n, f, a, b):
        total[f, 2 * n] = a
        total[f, 2 * n + 1] = b

    @pl.when(count > S)
    def _():
        weigh(1)
        lax.fori_loop(0, R // 2 // STEP, sweep(None, 1, keep), 0)

        @pl.when(count > 2 * S)
        def _():
            weigh(2)
            lax.fori_loop(0, R // 2 // STEP, sweep(total, 2, keep), 0)

        weigh(0)
        emit(sweep, total)

    @pl.when(count <= S)
    def _():
        weigh(0)
        emit(sweep, None)


def first_kernel(count, state, edge, got_x, got_y, ycat, bcat, locs, out, col_w, total, merged):
    lay_halos(got_x, got_y, merged)

    def row_of(f, i, odd):
        halo = pltpu.roll(merged[odd], lax.rem(2 * C - (f * R + i), C), 1)
        return state[f, i] + halo * edge[pl.ds(i, 1), :]

    def emit(sweep, base):
        def put(n, f, a, b):
            out[f, 2 * n] = a
            out[f, 2 * n + 1] = b

        lax.fori_loop(0, R // 2 // STEP, sweep(base, 0, put), 0)

    sweeps(row_of, count[0], ycat, bcat, locs, col_w, total, emit)


def second_kernel(own, got_x, got_y, state, out, buf, sem, ycat, bcat, locs, col_w, total):
    parts = []
    for index, raw in enumerate((own, got_x, got_y)):
        t = raw[...]
        rows = (t[GAIN : GAIN + 1], t[INNOV : INNOV + 1], t[ALPHA : ALPHA + 1])
        parts.append(choose(index, raw, t[:M], *rows))
    rank, count = ranks([a for _, a in parts])
    fields = jnp.concatenate([a for a, _ in parts], axis=1)
    compact_all(fields, jnp.concatenate(rank, axis=1), count, ycat, bcat, locs)

    def copy(ib, f):
        return pltpu.make_async_copy(
            buf.at[ib, f], out.at[f, :, pl.ds(ib * 8, 8), :], sem.at[ib, f]
        )

    def emit(sweep, base):
        for ib in range(R // 8):

            def put(n, f, a, b):
                rows = buf.at[ib, f].reshape(M * 8, C)
                r = 2 * (n - 4 * ib)
                rows[pl.ds(r, M, stride=8), :] = a
                rows[pl.ds(r + 1, M, stride=8), :] = b

            lax.fori_loop(4 * ib // STEP, (4 * ib + 4) // STEP, sweep(base, 0, put), 0)
            for f in range(F):
                copy(ib, f).start()

    sweeps(lambda f, i, odd: state[f, i], count, ycat, bcat, locs, col_w, total, emit)
    for ib in range(R // 8):
        for f in range(F):
            copy(ib, f).wait()


def call(kernel, outs, args, scratch=(), scalars=0, hbm=(), out_spaces=None, us=2, limit=24):
    spaces = [
        pltpu.SMEM if n < scalars else pltpu.HBM if n in hbm else VMEM for n in range(len(args))
    ]
    args = [
        pltpu.with_memory_space_constraint(a, s) if a.size > 100000 or s == pltpu.HBM else a
        for a, s in zip(args, spaces)
    ]
    out_spaces = out_spaces or [VMEM] * len(outs)
    return pl.pallas_call(
        kernel,
        out_shape=outs,
        in_specs=[pl.BlockSpec(memory_space=s) for s in spaces],
        out_specs=[pl.BlockSpec(memory_space=s) for s in out_spaces],
        scratch_shapes=scratch,
        compiler_params=pltpu.CompilerParams(vmem_limit_bytes=limit * MiB),
        cost_estimate=pl.CostEstimate(flops=0, transcendentals=0, bytes_accessed=us * 3000000),
        name=kernel.__name__,
    )(*args)


def swap(x, axis, shift):
    n = lax.axis_size(axis)
    pairs = [(i, ((i - shift) ^ 1) + shift) for i in range(n)]
    pairs = [(i, j) for i, j in pairs if i >= shift and 0 <= j < n]
    return lax.ppermute(x, axis, pairs)


def on_device(
    ensemble, courant_cols, courant_rows, obs_value, obs_error, obs_cell, obs_kind, obs_live, obs_list
):
    listed = jnp.transpose(obs_list, (2, 0, 1))
    block = VMEM((F, R, M, C), f32)
    sds = jax.ShapeDtypeStruct
    copies = [VMEM((R // 8, F, M, 8, C), f32)]
    sems = pltpu.SemaphoreType.DMA((R // 8, F))

    small = [
        obs_cell, obs_kind, courant_cols, courant_rows, obs_value, obs_error, obs_live, listed
    ]
    held = [(pltpu.SMEM if n < 2 else VMEM)(a.shape, a.dtype) for n, a in enumerate(small)]
    held_sems = pltpu.SemaphoreType.DMA((len(small),))

    pay_shape = sds((5 * M + T, C), f32)
    xt, pay_a, pay_b = call(
        edges_kernel,
        [block, pay_shape, pay_shape],
        [ensemble, *small],
        [*held, *copies, VMEM((3, T, C), f32), sems, held_sems],
        hbm=range(9),
    )
    got_b, got_a = swap(pay_b, "lat", 1), swap(pay_a, "lat", 0)
    later = call(
        later_kernel, [sds((T, C), f32)], [xt, *small], [*held, held_sems], hbm=range(1, 9), us=1
    )[0]
    lon_shape = sds((3 * M + T, C), f32)
    out_a, out_b = call(rows_kernel, [lon_shape] * 2, [xt, pay_a, later, got_a, got_b])
    got_y, got_x = swap(out_b, "lon", 1), swap(out_a, "lon", 0)
    state, edge = call(
        advect_kernel,
        [block, sds((R, C), f32)],
        [xt, got_a, got_b, courant_cols, courant_rows],
        [held[2], held[3], pltpu.SemaphoreType.DMA((2,))],
        hbm=(3, 4),
    )
    chosen = [sds((3, S, 2 * C), bf16), sds((3, M, 2 * C), bf16), sds((3, 3, S, C), f32)]
    table, count, *picked = call(
        tables_kernel,
        [sds((T, C), f32), sds((1,), jnp.int32), *chosen],
        [pay_a, got_a, got_b, out_a, got_x, got_y, edge],
        out_spaces=[VMEM, pltpu.SMEM, VMEM, VMEM, VMEM],
    )
    tab_b, tab_a = swap(table, "lat", 1), swap(table, "lat", 0)
    column = call(combine_kernel, [sds((T, C), f32)], [table, tab_a, tab_b], us=1)[0]
    col_y, col_x = swap(column, "lon", 1), swap(column, "lon", 0)
    work = [VMEM((S, C), f32), VMEM((F, R, M, C), f32)]
    state = call(
        first_kernel,
        [block],
        [count, state, edge, got_x, got_y, *picked],
        work + [VMEM((2, M, C), f32)],
        scalars=1,
        us=4,
    )[0]
    return call(
        second_kernel,
        [sds((F, M, R, C), f32)],
        [column, col_x, col_y, state],
        [*copies, sems]
        + [VMEM((3, S, 2 * C), bf16), VMEM((3, M, 2 * C), bf16), VMEM((3, 3, S, C), f32)]
        + work,
        out_spaces=[pltpu.HBM],
        us=6,
    )[0]


def solution(mesh):
    tiles = P(None, ("lat", "lon"))
    placed = (
        P(None, None, "lat", "lon"),
        P(None, "lat", "lon"),
        P(None, "lat", "lon"),
        tiles,
        tiles,
        tiles,
        tiles,
        tiles,
        P(None, ("lat", "lon"), None),
    )
    return jax.shard_map(
        on_device,
        mesh=mesh,
        in_specs=placed,
        out_specs=P(None, None, "lat", "lon"),
        check_vma=False,
    )
```

```python
import jax
import jax.numpy as jnp
from jax import lax
from jax.experimental import pallas as pl
from jax.experimental.pallas import tpu as pltpu
from jax.sharding import PartitionSpec as P

F, M, R, C, K = 3, 80, 32, 128, 24
GAIN, INNOV, ALPHA, ROW, COL, KIND = 80, 81, 82, 83, 84, 85
AE, AW, AN, AS, LIST, T = 88, 89, 90, 91, 96, 112
VALUE, ERROR, LIVE = GAIN, INNOV, ALPHA
SPARE = 96
LATER = 96
S = 80
STEP = 4
f32, bf16 = jnp.float32, jnp.bfloat16
VMEM = pltpu.VMEM
MiB = 1 << 20


def lanes(shape):
    return lax.broadcasted_iota(jnp.int32, shape, len(shape) - 1)


def split(x):
    hi = x.astype(bf16)
    return hi, (x - hi.astype(f32)).astype(bf16)


def dot(a, b, dims=((1,), (0,))):
    return lax.dot_general(a, b, (dims, ((), ())), preferred_element_type=f32)


def subs(shape):
    return lax.broadcasted_iota(jnp.int32, shape, 0)


def parity(axis):
    return lax.rem(lax.axis_index(axis), 2)


def flag(value, shape):
    return (jnp.zeros(shape, jnp.int32) + value) == 1


def stencil(u, v):
    uu, vv = 0.5 * u * u, 0.5 * v * v
    return 1.0 - 2.0 * uu - 2.0 * vv, uu - 0.5 * u, uu + 0.5 * u, vv - 0.5 * v, vv + 0.5 * v


def own_part(b, start, xt, cell, kind, cc, cr, value, error, live, listed, part):
    lane, lane1, lane8 = lanes((M, C)), lanes((1, C)), lanes((8, C))
    sub8 = subs((8, C))
    zero = jnp.zeros((1, C), f32)
    prior = jnp.zeros((M, C), f32)
    coefs = jnp.zeros((8, C), f32)
    rows = [zero] * 3
    for s in range(K):
        at = cell[b, s]
        r, c = lax.shift_right_logical(at, 7), lax.bitwise_and(at, C - 1)
        f = kind[b, s]
        rf = zero + r.astype(f32)
        mine1 = lane1 == start + s
        fields = (rf, zero + c.astype(f32), zero + f.astype(f32))
        rows = [jnp.where(mine1, w, old) for w, old in zip(fields, rows)]
        here, ae, aw, an, as_ = (
            jnp.where(lane1 == c, w, 0.0)
            for w in stencil(cc[0, pl.ds(r, 1), :], cr[0, pl.ds(r, 1), :])
        )
        stack = jnp.where(
            sub8 == 0, ae, jnp.where(sub8 == 1, aw, jnp.where(sub8 == 2, an, as_))
        )
        total = jnp.sum(stack, axis=1, keepdims=True)
        coefs = jnp.where(lane8 == start + s, total, coefs)
        ae = pltpu.roll(jnp.where(lane1 == C - 1, 0.0, ae), 1, 1)
        aw = pltpu.roll(jnp.where(lane1 == 0, 0.0, aw), C - 1, 1)
        an = jnp.where(rf == R - 1.0, 0.0, an)
        as_ = jnp.where(rf == 0.0, 0.0, as_)
        y = (here + ae + aw) * xt[f, r]
        y = y + an * xt[f, jnp.minimum(r + 1, R - 1)] + as_ * xt[f, jnp.maximum(r - 1, 0)]
        prior = jnp.where(lane == start + s, jnp.sum(y, axis=1, keepdims=True), prior)
    part[...] = jnp.zeros((T, C), f32)
    part[:M] = prior
    for n, w in zip((ROW, COL, KIND), rows):
        part[n : n + 1, :] = w
    part[AE : AE + 8, :] = coefs
    keep = slice(start, start + K)
    part[VALUE : VALUE + 1, keep] = value[b : b + 1, :]
    part[ERROR : ERROR + 1, keep] = error[b : b + 1, :]
    part[LIVE : LIVE + 1, keep] = live[b : b + 1, :].astype(f32)
    for n in range(9):
        part[LIST + n : LIST + n + 1, keep] = listed[n, b : b + 1, :].astype(f32)


def small_copies(srcs, dsts, sems):
    return [pltpu.make_async_copy(a, b, sems.at[n]) for n, (a, b) in enumerate(zip(srcs, dsts))]


def edges_kernel(*refs):
    x_hbm, small = refs[0], refs[1:9]
    xt, pay_a, pay_b = refs[9:12]
    here = refs[12:20]
    buf, acc, sem, small_sem = refs[20:]
    for ib in range(R // 8):
        for f in range(F):
            pltpu.make_async_copy(
                x_hbm.at[f, :, pl.ds(ib * 8, 8), :], buf.at[ib, f], sem.at[ib, f]
            ).start()
    copies = small_copies(small, here, small_sem)
    for c in copies:
        c.start()
    acc[...] = jnp.zeros_like(acc)
    lane = lanes((M, C))
    for ib in range(R // 8):
        for f in range(F):
            pltpu.make_async_copy(
                x_hbm.at[f, :, pl.ds(ib * 8, 8), :], buf.at[ib, f], sem.at[ib, f]
            ).wait()
            rows = buf.at[ib, f].reshape(M * 8, C)
            first, last = acc[0, :M], acc[1, :M]
            for r in range(8):
                v = rows[pl.ds(r, M, stride=8), :]
                i = ib * 8 + r
                k = f * R + i
                xt[f, i] = v
                turned = pltpu.roll(v, k, 1) if k else v
                first = jnp.where(lane == k, turned, first)
                last = jnp.where(lane == (k - 1) % C, turned, last)
            acc[0, :M] = first
            acc[1, :M] = last
    first, last = acc[0, :M], pltpu.roll(acc[1, :M], 1, 1)
    ra = jnp.where(parity("lat") == 1, 0, R - 1)
    rb = R - 1 - ra
    for f in range(F):
        pay_a[pl.ds(f * M, M), :] = xt[f, ra]
        pay_b[pl.ds(f * M, M), :] = xt[f, rb]
    for c in copies:
        c.wait()
    part = acc.at[2]
    own_part(0, SPARE, xt, *here, part)
    first = first + part[:M]
    for pay in (pay_a, pay_b):
        pay[pl.ds(F * M, M), :] = first
        pay[pl.ds(F * M + M, M), :] = last
        pay[pl.ds(5 * M, T - M), :] = part[M:]


def later_kernel(*refs):
    xt, small, out, here, small_sem = refs[0], refs[1:9], refs[9], refs[10:18], refs[18]
    copies = small_copies(small, here, small_sem)
    for c in copies:
        c.start()
    for c in copies:
        c.wait()
    own_part(1, LATER, xt, *here, out)


def combine(own, a, b):
    few = lanes((T, C)) < K
    return (
        own
        + pltpu.roll(jnp.where(few, a, 0.0), K, 1)
        + pltpu.roll(jnp.where(few, b, 0.0), 2 * K, 1)
    )


def lane_group():
    lane = lanes((1, C))
    group = jnp.where(lane < 2 * K, 1, jnp.where(lane < 3 * K, 2, 3))
    return jnp.where((lane < K) | ((lane >= LATER) & (lane < LATER + K)), 0, group)


def pickup(sources, key):
    hot = (subs((F * C, C)).astype(f32) == key).astype(f32).astype(bf16)
    return sum(dot(h, hot) for h in split(jnp.concatenate(sources, axis=1)))


def spare_only(x):
    lane = lanes(x.shape)
    return jnp.where((lane >= SPARE) & (lane < SPARE + K), x, 0.0)


def rows_kernel(xt, pay, later, got_a, got_b, out_a, out_b, own):
    pa, pb = parity("lat"), parity("lon")
    comb = later[...]
    for n, src in enumerate((pay, got_a, got_b)):
        part = jnp.concatenate([src[pl.ds(F * M, M), :], src[pl.ds(5 * M, T - M), :]], axis=0)
        comb = comb + pltpu.roll(spare_only(part), C - SPARE + n * K, 1)
    row, col, kind = comb[ROW : ROW + 1], comb[COL : COL + 1], comb[KIND : KIND + 1]
    group = lane_group()
    edge_a = jnp.where(pa == 1, 0, R - 1)
    edge_b = R - 1 - edge_a
    cellkey = kind * C + col

    def key(n, edge):
        return jnp.where((group == n) & (row == edge.astype(f32)), cellkey, -1.0)

    total = pickup([got_a[pl.ds(f * M, M), :] for f in range(F)], key(0, edge_a))
    total += pickup([got_b[pl.ds(f * M, M), :] for f in range(F)], key(0, edge_b))
    total += pickup([xt[f, edge_a] for f in range(F)], key(1, edge_b))
    total += pickup([xt[f, edge_b] for f in range(F)], key(2, edge_a))
    coef = jnp.where(row == 0.0, comb[AS : AS + 1], comb[AN : AN + 1])
    prior = comb[:M] + coef * total
    odd = flag(pb, (M, C))
    for n, src in enumerate((pay, got_a, got_b)):
        first, last = src[pl.ds(F * M, M), :], src[pl.ds(F * M + M, M), :]
        column = lanes((M, C)) < SPARE
        mine = spare_only(pltpu.roll(prior, SPARE - n * K, 1))
        out_a[pl.ds(n * M, M), :] = jnp.where(column, jnp.where(odd, first, last), mine)
        out_b[pl.ds(n * M, M), :] = jnp.where(column, jnp.where(odd, last, first), mine)
    for out in (out_a, out_b):
        out[pl.ds(3 * M, T - M), :] = comb[M:]
    own[:M] = prior
    own[M:] = comb[M:]


def statistics(t):
    prior = t[:M]
    ybar = jnp.sum(prior, axis=0, keepdims=True) / M
    yp = prior - ybar
    spread = jnp.sum(yp * yp, axis=0, keepdims=True) / (M - 1)
    err = t[ERROR : ERROR + 1]
    total = spread + err
    total = jnp.where(total == 0.0, 1.0, total)
    gain = t[LIVE : LIVE + 1] / total
    alpha = 1.0 / (1.0 + jnp.sqrt(err / total))
    innov = t[VALUE : VALUE + 1] - ybar
    return yp, gain, innov, alpha


def stack_fields(yp, rows):
    sub = subs((16, C))
    extra = jnp.zeros((16, C), f32)
    for n, v in enumerate(rows):
        extra = jnp.where(sub == n, v, extra)
    return jnp.concatenate([yp, extra], axis=0)


def choose(index, raw, yp, gain, innov, alpha):
    sa = 1 - 2 * parity("lat")
    sb = 1 - 2 * parity("lon")
    db = (0, sb, -sb)[index]
    group = lane_group()
    chosen = jnp.zeros((1, C), f32)
    row = raw[ROW : ROW + 1, :]
    for n, da in enumerate((0, sa, -sa)):
        listed = raw[pl.ds(LIST + (1 - da) * 3 + (1 - db), 1), :]
        chosen = jnp.where(group == n, listed, chosen)
        row = jnp.where(group == n, row + jnp.asarray(da * R, f32), row)
    col = raw[COL : COL + 1, :] + jnp.asarray(db * C, f32)
    factor = gain * chosen
    near = (row > -float(R)) & (row < 2.0 * R - 1.0) & (col > -float(R)) & (col < C + R - 1.0)
    act = near & (factor != 0.0) & (lanes((1, C)) < 3 * K)
    return stack_fields(yp, (factor, innov, alpha, row, col)), jnp.where(act, 1.0, 0.0)


def ranks(actives):
    before = (subs((C, C)) < lanes((C, C))).astype(f32).astype(bf16)
    out, offset = [], jnp.zeros((1, 1), f32)
    for act in actives:
        r = dot(jnp.broadcast_to(act, (8, C)).astype(bf16), before)[:1] + offset
        out.append(jnp.where(act > 0.0, r, -1.0))
        offset = offset + jnp.sum(act, axis=1, keepdims=True)
    return out, sum(jnp.sum(a) for a in actives).astype(jnp.int32)


def spread_lanes(hi, lo):
    r = lax.broadcasted_iota(jnp.int32, (C, 2 * C), 0)
    c = lax.broadcasted_iota(jnp.int32, (C, 2 * C), 1)
    keep = r < S
    e_hi = (((c == r) | (c == r + 2 * S)) & keep).astype(f32).astype(bf16)
    e_lo = ((c == r + S) & keep).astype(f32).astype(bf16)
    return (dot(hi, e_hi) + dot(lo, e_lo)).astype(bf16)


def compact(fields, rank, chunk, ycat, bcat, locs):
    p = subs((C, F * C)).astype(f32) + jnp.asarray(chunk * S, f32)
    own = subs((C, F * C)) < S
    pick = ((rank == p) & own).astype(f32).astype(bf16)
    turned = sum(dot(t, pick, ((1,), (1,))) for t in split(fields))
    chosen = jnp.concatenate([turned, jnp.zeros((32, C), f32)], axis=0).T[:S]
    ycat[chunk] = spread_lanes(*split(chosen))
    back = turned[INNOV : INNOV + 1, :] - turned[ALPHA : ALPHA + 1, :] * turned[:M]
    bcat[chunk] = spread_lanes(*split(back))
    locs[chunk, 0] = jnp.broadcast_to(chosen[:, ROW : ROW + 1], (S, C))
    locs[chunk, 1] = jnp.broadcast_to(chosen[:, COL : COL + 1], (S, C))
    locs[chunk, 2] = jnp.broadcast_to(chosen[:, GAIN : GAIN + 1], (S, C)) / (M - 1)


def compact_all(fields, rank, count, ycat, bcat, locs):
    compact(fields, rank, 0, ycat, bcat, locs)

    @pl.when(count > S)
    def _():
        def body(j, carry):
            compact(fields, rank, j, ycat, bcat, locs)
            return carry

        lax.fori_loop(1, (count + S - 1) // S, body, 0)


def taper(d):
    z = jnp.maximum(0.0, 1.0 - jnp.abs(d) / R)
    return z * z


def update(p, lw, ycat, bcat):
    hi, lo = split(p)
    none = jnp.zeros((2 * C - 3 * M, p.shape[1]), bf16)
    proj = dot(ycat, jnp.concatenate([hi, hi, lo, none], axis=0))
    hi, lo = split(proj * lw)
    return dot(bcat, jnp.concatenate([hi, hi, lo, none], axis=0))


def tables_kernel(
    pay, got_a, got_b, own_in, got_x, got_y, after, table, count_out, ycat, bcat, locs, sides
):
    pb = parity("lon")
    edge_x = jnp.where(pb == 1, 0.0, C - 1.0)
    edge_y = C - 1.0 - edge_x
    group = lane_group()
    odd = flag(pb, (M, C))
    mine_x, mine_y = [], []
    for src in (pay, got_a, got_b):
        first, last = src[pl.ds(F * M, M), :], src[pl.ds(F * M + M, M), :]
        mine_x.append(jnp.where(odd, first, last))
        mine_y.append(jnp.where(odd, last, first))

    def complete(t, parts):
        row, col, kind = t[ROW : ROW + 1], t[COL : COL + 1], t[KIND : KIND + 1]
        at = group.astype(f32) * C + kind * R + row
        total = jnp.zeros((M, C), f32)
        for packs, edge in parts:
            total += pickup(packs, jnp.where((group < 3) & (col == edge), at, -1.0))
        coef = jnp.where(col == 0.0, t[AW : AW + 1], t[AE : AE + 1])
        return t[:M] + coef * total

    def packs(got):
        return [got[pl.ds(n * M, M), :] for n in range(3)]

    for side, got in enumerate((got_x, got_y)):
        sides[side, :M] = sum(
            pltpu.roll(spare_only(h), C - SPARE + n * K, 1) for n, h in enumerate(packs(got))
        )
        sides[side, M:] = got[pl.ds(3 * M, T - M), :]
    out = []
    later = None
    for index, (src, parts) in enumerate((
        (own_in, ((packs(got_x), edge_x), (packs(got_y), edge_y))),
        (sides.at[0], ((mine_x, edge_y),)),
        (sides.at[1], ((mine_y, edge_x),)),
    )):
        raw = src
        t = raw[...]
        whole = jnp.concatenate([complete(t, parts), t[M:]], axis=0)
        if index == 0:
            later = whole
        out.append(choose(index, raw, *statistics(whole)))
    fields = jnp.concatenate([a for a, _ in out], axis=1)
    rank, count = ranks([a for _, a in out])
    rank = jnp.concatenate(rank, axis=1)
    count_out[0] = count
    compact_all(fields, rank, count, ycat, bcat, locs)

    prior = later[:M]
    row, col = later[ROW : ROW + 1], later[COL : COL + 1]

    def point(j, add):
        lw = taper(locs[j, 0] - row) * taper(locs[j, 1] - col) * locs[j, 2]
        return add + update(prior, lw, ycat[j], bcat[j])

    add = lax.fori_loop(0, jnp.maximum((count + S - 1) // S, 1), point, jnp.zeros((M, C), f32))
    later = jnp.concatenate([prior + add, later[M:]], axis=0)
    yp, gain, innov, alpha = statistics(later)
    fresh = stack_fields(yp, (gain, innov, alpha, row, col))
    fresh = jnp.concatenate([fresh, later[LIST:]], axis=0)
    lane = lanes((T, C))
    fresh = jnp.where((lane >= LATER) & (lane < LATER + K), fresh, 0.0)
    table[...] = pltpu.roll(fresh, C - LATER, 1)


def combine_kernel(own, a, b, out):
    out[...] = combine(own[...], a[...], b[...])


def advect_kernel(xt, got_a, got_b, cc_hbm, cr_hbm, state, edge, cc, cr, sems):
    copies = small_copies((cc_hbm, cr_hbm), (cc, cr), sems)
    for c in copies:
        c.start()
    for c in copies:
        c.wait()
    lane1 = lanes((1, C))
    odd_a = flag(parity("lat"), (M, C))

    def one(i, low, high):
        here, ae, aw, an, as_ = stencil(cc[0, pl.ds(i, 1), :], cr[0, pl.ds(i, 1), :])
        edge[pl.ds(i, 1), :] = jnp.where(
            lane1 == 0, aw, jnp.where(lane1 == C - 1, ae, 0.0)
        )
        ae = jnp.where(lane1 == C - 1, 0.0, ae)
        aw = jnp.where(lane1 == 0, 0.0, aw)
        for f in range(F):
            x = xt[f, i]
            ha, hb = got_a[pl.ds(f * M, M), :], got_b[pl.ds(f * M, M), :]
            xs = jnp.where(odd_a, ha, hb) if low else xt[f, i - 1]
            xn = jnp.where(odd_a, hb, ha) if high else xt[f, i + 1]
            y = here * x + ae * pltpu.roll(x, C - 1, 1) + aw * pltpu.roll(x, 1, 1)
            state[f, i] = y + an * xn + as_ * xs

    one(0, True, False)
    one(R - 1, False, True)

    def body(n, carry):
        one(2 * n + 1, False, False)
        one(2 * n + 2, False, False)
        return carry

    lax.fori_loop(0, R // 2 - 1, body, 0)


def lay_halos(got_x, got_y, merged):
    odd_lane = (lanes((M, C)) % 2) == 1
    odd_b = flag(parity("lon"), (M, C))
    got_1, got_2 = got_x[pl.ds(0, M), :], got_y[pl.ds(0, M), :]
    east = pltpu.roll(jnp.where(odd_b, got_2, got_1), C - 1, 1)
    west = jnp.where(odd_b, got_1, got_2)
    merged[0] = jnp.where(odd_lane, east, west)
    merged[1] = jnp.where(odd_lane, west, east)


def sweeps(row_of, count, ycat, bcat, locs, row_w, col_w, total, emit):
    def weigh(j):
        row_w[...] = taper(locs[j, 0] - lanes((S, C)).astype(f32))
        col_w[...] = taper(locs[j, 1] - lanes((S, C)).astype(f32)) * locs[j, 2]

    def sweep(base, j, put):
        def local(i):
            if isinstance(i, int):
                return jnp.broadcast_to(row_w[:, i : i + 1], (S, C)) * col_w[...]
            return taper(locs[j, 0] - i.astype(f32)) * col_w[...]

        def body(step, carry):
            for n in [step * STEP + u for u in range(STEP)]:
                i = 2 * n
                lw = jnp.concatenate([local(i), local(i + 1)], axis=1)
                for f in range(F):
                    pair = row_of(f, i, 0), row_of(f, i + 1, 1)
                    d = update(jnp.concatenate(pair, axis=1), lw, ycat[j], bcat[j])
                    if base is not None:
                        pair = base[f, i], base[f, i + 1]
                    put(n, f, pair[0] + d[:, :C], pair[1] + d[:, C:])
            return carry

        return body

    def keep(n, f, a, b):
        total[f, 2 * n] = a
        total[f, 2 * n + 1] = b

    @pl.when(count > S)
    def _():
        weigh(1)
        lax.fori_loop(0, R // 2 // STEP, sweep(None, 1, keep), 0)

        @pl.when(count > 2 * S)
        def _():
            weigh(2)
            lax.fori_loop(0, R // 2 // STEP, sweep(total, 2, keep), 0)

        weigh(0)
        emit(sweep, total)

    @pl.when(count <= S)
    def _():
        weigh(0)
        emit(sweep, None)


def first_kernel(count, state, edge, got_x, got_y, ycat, bcat, locs, out, row_w, col_w, total, merged):
    lay_halos(got_x, got_y, merged)

    def row_of(f, i, odd):
        halo = pltpu.roll(merged[odd], lax.rem(2 * C - (f * R + i), C), 1)
        return state[f, i] + halo * edge[pl.ds(i, 1), :]

    def emit(sweep, base):
        def put(n, f, a, b):
            out[f, 2 * n] = a
            out[f, 2 * n + 1] = b

        lax.fori_loop(0, R // 2 // STEP, sweep(base, 0, put), 0)

    sweeps(row_of, count[0], ycat, bcat, locs, row_w, col_w, total, emit)


def second_kernel(own, got_x, got_y, state, out, buf, sem, ycat, bcat, locs, row_w, col_w, total):
    parts = []
    for index, raw in enumerate((own, got_x, got_y)):
        t = raw[...]
        rows = (t[GAIN : GAIN + 1], t[INNOV : INNOV + 1], t[ALPHA : ALPHA + 1])
        parts.append(choose(index, raw, t[:M], *rows))
    rank, count = ranks([a for _, a in parts])
    fields = jnp.concatenate([a for a, _ in parts], axis=1)
    compact_all(fields, jnp.concatenate(rank, axis=1), count, ycat, bcat, locs)

    def copy(ib, f):
        return pltpu.make_async_copy(
            buf.at[ib, f], out.at[f, :, pl.ds(ib * 8, 8), :], sem.at[ib, f]
        )

    def emit(sweep, base):
        for ib in range(R // 8):

            def put(n, f, a, b):
                rows = buf.at[ib, f].reshape(M * 8, C)
                r = 2 * (n - 4 * ib)
                rows[pl.ds(r, M, stride=8), :] = a
                rows[pl.ds(r + 1, M, stride=8), :] = b

            for step in range(4 * ib // STEP, (4 * ib + 4) // STEP):
                sweep(base, 0, put)(step, 0)
            for f in range(F):
                copy(ib, f).start()

    sweeps(lambda f, i, odd: state[f, i], count, ycat, bcat, locs, row_w, col_w, total, emit)
    for ib in range(R // 8):
        for f in range(F):
            copy(ib, f).wait()


def call(kernel, outs, args, scratch=(), scalars=0, hbm=(), out_spaces=None, us=2, limit=24):
    spaces = [
        pltpu.SMEM if n < scalars else pltpu.HBM if n in hbm else VMEM for n in range(len(args))
    ]
    args = [
        pltpu.with_memory_space_constraint(a, s) if a.size > 100000 or s == pltpu.HBM else a
        for a, s in zip(args, spaces)
    ]
    out_spaces = out_spaces or [VMEM] * len(outs)
    return pl.pallas_call(
        kernel,
        out_shape=outs,
        in_specs=[pl.BlockSpec(memory_space=s) for s in spaces],
        out_specs=[pl.BlockSpec(memory_space=s) for s in out_spaces],
        scratch_shapes=scratch,
        compiler_params=pltpu.CompilerParams(vmem_limit_bytes=limit * MiB),
        cost_estimate=pl.CostEstimate(flops=0, transcendentals=0, bytes_accessed=us * 3000000),
        name=kernel.__name__,
    )(*args)


def swap(x, axis, shift):
    n = lax.axis_size(axis)
    pairs = [(i, ((i - shift) ^ 1) + shift) for i in range(n)]
    pairs = [(i, j) for i, j in pairs if i >= shift and 0 <= j < n]
    return lax.ppermute(x, axis, pairs)


def on_device(
    ensemble, courant_cols, courant_rows, obs_value, obs_error, obs_cell, obs_kind, obs_live, obs_list
):
    listed = jnp.transpose(obs_list, (2, 0, 1))
    block = VMEM((F, R, M, C), f32)
    sds = jax.ShapeDtypeStruct
    copies = [VMEM((R // 8, F, M, 8, C), f32)]
    sems = pltpu.SemaphoreType.DMA((R // 8, F))

    small = [
        obs_cell, obs_kind, courant_cols, courant_rows, obs_value, obs_error, obs_live, listed
    ]
    held = [(pltpu.SMEM if n < 2 else VMEM)(a.shape, a.dtype) for n, a in enumerate(small)]
    held_sems = pltpu.SemaphoreType.DMA((len(small),))

    pay_shape = sds((4 * M + T, C), f32)
    xt, pay_a, pay_b = call(
        edges_kernel,
        [block, pay_shape, pay_shape],
        [ensemble, *small],
        [*held, *copies, VMEM((3, T, C), f32), sems, held_sems],
        hbm=range(9),
    )
    got_b, got_a = swap(pay_b, "lat", 1), swap(pay_a, "lat", 0)
    later = call(
        later_kernel, [sds((T, C), f32)], [xt, *small], [*held, held_sems], hbm=range(1, 9), us=1
    )[0]
    lon_shape = sds((2 * M + T, C), f32)
    out_a, out_b, own = call(
        rows_kernel, [lon_shape] * 2 + [sds((T, C), f32)], [xt, pay_a, later, got_a, got_b]
    )
    got_y, got_x = swap(out_b, "lon", 1), swap(out_a, "lon", 0)
    state, edge = call(
        advect_kernel,
        [block, sds((R, C), f32)],
        [xt, got_a, got_b, courant_cols, courant_rows],
        [held[2], held[3], pltpu.SemaphoreType.DMA((2,))],
        hbm=(3, 4),
    )
    chosen = [sds((3, S, 2 * C), bf16), sds((3, M, 2 * C), bf16), sds((3, 3, S, C), f32)]
    table, count, *picked = call(
        tables_kernel,
        [sds((T, C), f32), sds((1,), jnp.int32), *chosen],
        [pay_a, got_a, got_b, own, got_x, got_y, edge],
        [VMEM((2, T, C), f32)],
        out_spaces=[VMEM, pltpu.SMEM, VMEM, VMEM, VMEM],
    )
    tab_b, tab_a = swap(table, "lat", 1), swap(table, "lat", 0)
    column = call(combine_kernel, [sds((T, C), f32)], [table, tab_a, tab_b], us=1)[0]
    col_y, col_x = swap(column, "lon", 1), swap(column, "lon", 0)
    work = [VMEM((S, C), f32), VMEM((S, C), f32), VMEM((F, R, M, C), f32)]
    state = call(
        first_kernel,
        [block],
        [count, state, edge, got_x, got_y, *picked],
        work + [VMEM((2, M, C), f32)],
        scalars=1,
        us=4,
    )[0]
    return call(
        second_kernel,
        [sds((F, M, R, C), f32)],
        [column, col_x, col_y, state],
        [*copies, sems]
        + [VMEM((3, S, 2 * C), bf16), VMEM((3, M, 2 * C), bf16), VMEM((3, 3, S, C), f32)]
        + work,
        out_spaces=[pltpu.HBM],
        us=6,
    )[0]


def solution(mesh):
    tiles = P(None, ("lat", "lon"))
    placed = (
        P(None, None, "lat", "lon"),
        P(None, "lat", "lon"),
        P(None, "lat", "lon"),
        tiles,
        tiles,
        tiles,
        tiles,
        tiles,
        P(None, ("lat", "lon"), None),
    )
    return jax.shard_map(
        on_device,
        mesh=mesh,
        in_specs=placed,
        out_specs=P(None, None, "lat", "lon"),
        check_vma=False,
    )
```

```python
import jax
import jax.numpy as jnp
from jax import lax
from jax.experimental import pallas as pl
from jax.experimental.pallas import tpu as pltpu
from jax.sharding import PartitionSpec as P

F, M, R, C, K = 3, 80, 32, 128, 24
GAIN, INNOV, ALPHA, ROW, COL, KIND = 80, 81, 82, 83, 84, 85
AE, AW, AN, AS, LIST, T = 88, 89, 90, 91, 96, 112
VALUE, ERROR, LIVE = GAIN, INNOV, ALPHA
SPARE = 96
LATER = 96
S = 80
STEP = 4
f32, bf16 = jnp.float32, jnp.bfloat16
VMEM = pltpu.VMEM
MiB = 1 << 20


def lanes(shape):
    return lax.broadcasted_iota(jnp.int32, shape, len(shape) - 1)


def split(x):
    hi = x.astype(bf16)
    return hi, (x - hi.astype(f32)).astype(bf16)


def dot(a, b, dims=((1,), (0,))):
    return lax.dot_general(a, b, (dims, ((), ())), preferred_element_type=f32)


def subs(shape):
    return lax.broadcasted_iota(jnp.int32, shape, 0)


def parity(axis):
    return lax.rem(lax.axis_index(axis), 2)


def flag(value, shape):
    return (jnp.zeros(shape, jnp.int32) + value) == 1


def stencil(u, v):
    uu, vv = 0.5 * u * u, 0.5 * v * v
    return 1.0 - 2.0 * uu - 2.0 * vv, uu - 0.5 * u, uu + 0.5 * u, vv - 0.5 * v, vv + 0.5 * v


def own_part(b, start, xt, cell, kind, cc, cr, value, error, live, listed, part):
    lane, lane1, lane8 = lanes((M, C)), lanes((1, C)), lanes((8, C))
    sub8 = subs((8, C))
    zero = jnp.zeros((1, C), f32)
    prior = jnp.zeros((M, C), f32)
    coefs = jnp.zeros((8, C), f32)
    rows = [zero] * 3
    for s in range(K):
        at = cell[b, s]
        r, c = lax.shift_right_logical(at, 7), lax.bitwise_and(at, C - 1)
        f = kind[b, s]
        rf = zero + r.astype(f32)
        mine1 = lane1 == start + s
        fields = (rf, zero + c.astype(f32), zero + f.astype(f32))
        rows = [jnp.where(mine1, w, old) for w, old in zip(fields, rows)]
        here, ae, aw, an, as_ = (
            jnp.where(lane1 == c, w, 0.0)
            for w in stencil(cc[0, pl.ds(r, 1), :], cr[0, pl.ds(r, 1), :])
        )
        stack = jnp.where(
            sub8 == 0, ae, jnp.where(sub8 == 1, aw, jnp.where(sub8 == 2, an, as_))
        )
        total = jnp.sum(stack, axis=1, keepdims=True)
        coefs = jnp.where(lane8 == start + s, total, coefs)
        ae = pltpu.roll(jnp.where(lane1 == C - 1, 0.0, ae), 1, 1)
        aw = pltpu.roll(jnp.where(lane1 == 0, 0.0, aw), C - 1, 1)
        an = jnp.where(rf == R - 1.0, 0.0, an)
        as_ = jnp.where(rf == 0.0, 0.0, as_)
        y = (here + ae + aw) * xt[f, r]
        y = y + an * xt[f, jnp.minimum(r + 1, R - 1)] + as_ * xt[f, jnp.maximum(r - 1, 0)]
        prior = jnp.where(lane == start + s, jnp.sum(y, axis=1, keepdims=True), prior)
    part[...] = jnp.zeros((T, C), f32)
    part[:M] = prior
    for n, w in zip((ROW, COL, KIND), rows):
        part[n : n + 1, :] = w
    part[AE : AE + 8, :] = coefs
    keep = slice(start, start + K)
    part[VALUE : VALUE + 1, keep] = value[b : b + 1, :]
    part[ERROR : ERROR + 1, keep] = error[b : b + 1, :]
    part[LIVE : LIVE + 1, keep] = live[b : b + 1, :].astype(f32)
    for n in range(9):
        part[LIST + n : LIST + n + 1, keep] = listed[n, b : b + 1, :].astype(f32)


def small_copies(srcs, dsts, sems):
    return [pltpu.make_async_copy(a, b, sems.at[n]) for n, (a, b) in enumerate(zip(srcs, dsts))]


def edges_kernel(*refs):
    x_hbm, small = refs[0], refs[1:9]
    xt, pay_a, pay_b = refs[9:12]
    here = refs[12:20]
    buf, acc, sem, small_sem = refs[20:]
    for ib in range(R // 8):
        for f in range(F):
            pltpu.make_async_copy(
                x_hbm.at[f, :, pl.ds(ib * 8, 8), :], buf.at[ib, f], sem.at[ib, f]
            ).start()
    copies = small_copies(small, here, small_sem)
    for c in copies:
        c.start()
    acc[...] = jnp.zeros_like(acc)
    lane = lanes((M, C))
    for ib in range(R // 8):
        for f in range(F):
            pltpu.make_async_copy(
                x_hbm.at[f, :, pl.ds(ib * 8, 8), :], buf.at[ib, f], sem.at[ib, f]
            ).wait()
            rows = buf.at[ib, f].reshape(M * 8, C)
            first, last = acc[0, :M], acc[1, :M]
            for r in range(8):
                v = rows[pl.ds(r, M, stride=8), :]
                i = ib * 8 + r
                k = f * R + i
                xt[f, i] = v
                turned = pltpu.roll(v, k, 1) if k else v
                first = jnp.where(lane == k, turned, first)
                last = jnp.where(lane == (k - 1) % C, turned, last)
            acc[0, :M] = first
            acc[1, :M] = last
    first, last = acc[0, :M], pltpu.roll(acc[1, :M], 1, 1)
    ra = jnp.where(parity("lat") == 1, 0, R - 1)
    rb = R - 1 - ra
    for f in range(F):
        pay_a[pl.ds(f * M, M), :] = xt[f, ra]
        pay_b[pl.ds(f * M, M), :] = xt[f, rb]
    for c in copies:
        c.wait()
    part = acc.at[2]
    own_part(0, SPARE, xt, *here, part)
    first = first + part[:M]
    for pay in (pay_a, pay_b):
        pay[pl.ds(F * M, M), :] = first
        pay[pl.ds(F * M + M, M), :] = last
        pay[pl.ds(5 * M, T - M), :] = part[M:]


def later_kernel(cell, kind, xt, *refs):
    own_part(1, LATER, xt, cell, kind, *refs)


def combine(own, a, b):
    few = lanes((T, C)) < K
    return (
        own
        + pltpu.roll(jnp.where(few, a, 0.0), K, 1)
        + pltpu.roll(jnp.where(few, b, 0.0), 2 * K, 1)
    )


def lane_group():
    lane = lanes((1, C))
    group = jnp.where(lane < 2 * K, 1, jnp.where(lane < 3 * K, 2, 3))
    return jnp.where((lane < K) | ((lane >= LATER) & (lane < LATER + K)), 0, group)


def pickup(sources, key):
    hot = (subs((F * C, C)).astype(f32) == key).astype(f32).astype(bf16)
    return sum(dot(h, hot) for h in split(jnp.concatenate(sources, axis=1)))


def spare_only(x):
    lane = lanes(x.shape)
    return jnp.where((lane >= SPARE) & (lane < SPARE + K), x, 0.0)


def rows_kernel(xt, pay, later, got_a, got_b, out_a, out_b, own):
    pa, pb = parity("lat"), parity("lon")
    comb = later[...]
    for n, src in enumerate((pay, got_a, got_b)):
        part = jnp.concatenate([src[pl.ds(F * M, M), :], src[pl.ds(5 * M, T - M), :]], axis=0)
        comb = comb + pltpu.roll(spare_only(part), C - SPARE + n * K, 1)
    row, col, kind = comb[ROW : ROW + 1], comb[COL : COL + 1], comb[KIND : KIND + 1]
    group = lane_group()
    edge_a = jnp.where(pa == 1, 0, R - 1)
    edge_b = R - 1 - edge_a
    cellkey = kind * C + col

    def key(n, edge):
        return jnp.where((group == n) & (row == edge.astype(f32)), cellkey, -1.0)

    total = pickup([got_a[pl.ds(f * M, M), :] for f in range(F)], key(0, edge_a))
    total += pickup([got_b[pl.ds(f * M, M), :] for f in range(F)], key(0, edge_b))
    total += pickup([xt[f, edge_a] for f in range(F)], key(1, edge_b))
    total += pickup([xt[f, edge_b] for f in range(F)], key(2, edge_a))
    coef = jnp.where(row == 0.0, comb[AS : AS + 1], comb[AN : AN + 1])
    prior = comb[:M] + coef * total
    odd = flag(pb, (M, C))
    for n, src in enumerate((pay, got_a, got_b)):
        first, last = src[pl.ds(F * M, M), :], src[pl.ds(F * M + M, M), :]
        column = lanes((M, C)) < SPARE
        mine = spare_only(pltpu.roll(prior, SPARE - n * K, 1))
        out_a[pl.ds(n * M, M), :] = jnp.where(column, jnp.where(odd, first, last), mine)
        out_b[pl.ds(n * M, M), :] = jnp.where(column, jnp.where(odd, last, first), mine)
    for out in (out_a, out_b):
        out[pl.ds(3 * M, T - M), :] = comb[M:]
    own[:M] = prior
    own[M:] = comb[M:]


def statistics(t):
    prior = t[:M]
    ybar = jnp.sum(prior, axis=0, keepdims=True) / M
    yp = prior - ybar
    spread = jnp.sum(yp * yp, axis=0, keepdims=True) / (M - 1)
    err = t[ERROR : ERROR + 1]
    total = spread + err
    total = jnp.where(total == 0.0, 1.0, total)
    gain = t[LIVE : LIVE + 1] / total
    alpha = 1.0 / (1.0 + jnp.sqrt(err / total))
    innov = t[VALUE : VALUE + 1] - ybar
    return yp, gain, innov, alpha


def stack_fields(yp, rows):
    sub = subs((16, C))
    extra = jnp.zeros((16, C), f32)
    for n, v in enumerate(rows):
        extra = jnp.where(sub == n, v, extra)
    return jnp.concatenate([yp, extra], axis=0)


def choose(index, raw, yp, gain, innov, alpha):
    sa = 1 - 2 * parity("lat")
    sb = 1 - 2 * parity("lon")
    db = (0, sb, -sb)[index]
    group = lane_group()
    chosen = jnp.zeros((1, C), f32)
    row = raw[ROW : ROW + 1, :]
    for n, da in enumerate((0, sa, -sa)):
        listed = raw[pl.ds(LIST + (1 - da) * 3 + (1 - db), 1), :]
        chosen = jnp.where(group == n, listed, chosen)
        row = jnp.where(group == n, row + jnp.asarray(da * R, f32), row)
    col = raw[COL : COL + 1, :] + jnp.asarray(db * C, f32)
    factor = gain * chosen
    near = (row > -float(R)) & (row < 2.0 * R - 1.0) & (col > -float(R)) & (col < C + R - 1.0)
    act = near & (factor != 0.0) & (lanes((1, C)) < 3 * K)
    return stack_fields(yp, (factor, innov, alpha, row, col)), jnp.where(act, 1.0, 0.0)


def ranks(actives):
    before = (subs((C, C)) < lanes((C, C))).astype(f32).astype(bf16)
    out, offset = [], jnp.zeros((1, 1), f32)
    for act in actives:
        r = dot(jnp.broadcast_to(act, (8, C)).astype(bf16), before)[:1] + offset
        out.append(jnp.where(act > 0.0, r, -1.0))
        offset = offset + jnp.sum(act, axis=1, keepdims=True)
    return out, sum(jnp.sum(a) for a in actives).astype(jnp.int32)


def spread_lanes(hi, lo):
    r = lax.broadcasted_iota(jnp.int32, (C, 2 * C), 0)
    c = lax.broadcasted_iota(jnp.int32, (C, 2 * C), 1)
    keep = r < S
    e_hi = (((c == r) | (c == r + 2 * S)) & keep).astype(f32).astype(bf16)
    e_lo = ((c == r + S) & keep).astype(f32).astype(bf16)
    return (dot(hi, e_hi) + dot(lo, e_lo)).astype(bf16)


def compact(fields, rank, chunk, ycat, bcat, locs):
    p = subs((C, F * C)).astype(f32) + jnp.asarray(chunk * S, f32)
    own = subs((C, F * C)) < S
    pick = ((rank == p) & own).astype(f32).astype(bf16)
    turned = sum(dot(t, pick, ((1,), (1,))) for t in split(fields))
    chosen = jnp.concatenate([turned, jnp.zeros((32, C), f32)], axis=0).T[:S]
    ycat[chunk] = spread_lanes(*split(chosen))
    back = turned[INNOV : INNOV + 1, :] - turned[ALPHA : ALPHA + 1, :] * turned[:M]
    bcat[chunk] = spread_lanes(*split(back))
    locs[chunk, 0] = jnp.broadcast_to(chosen[:, ROW : ROW + 1], (S, C))
    locs[chunk, 1] = jnp.broadcast_to(chosen[:, COL : COL + 1], (S, C))
    locs[chunk, 2] = jnp.broadcast_to(chosen[:, GAIN : GAIN + 1], (S, C)) / (M - 1)


def compact_all(fields, rank, count, ycat, bcat, locs):
    compact(fields, rank, 0, ycat, bcat, locs)

    @pl.when(count > S)
    def _():
        def body(j, carry):
            compact(fields, rank, j, ycat, bcat, locs)
            return carry

        lax.fori_loop(1, (count + S - 1) // S, body, 0)


def taper(d):
    z = jnp.maximum(0.0, 1.0 - jnp.abs(d) / R)
    return z * z


def update(p, lw, ycat, bcat):
    hi, lo = split(p)
    none = jnp.zeros((2 * C - 3 * M, p.shape[1]), bf16)
    proj = dot(ycat, jnp.concatenate([hi, hi, lo, none], axis=0))
    hi, lo = split(proj * lw)
    return dot(bcat, jnp.concatenate([hi, hi, lo, none], axis=0))


def tables_kernel(
    pay, got_a, got_b, own_in, got_x, got_y, after, table, count_out, ycat, bcat, locs, sides
):
    pb = parity("lon")
    edge_x = jnp.where(pb == 1, 0.0, C - 1.0)
    edge_y = C - 1.0 - edge_x
    group = lane_group()
    odd = flag(pb, (M, C))
    mine_x, mine_y = [], []
    for src in (pay, got_a, got_b):
        first, last = src[pl.ds(F * M, M), :], src[pl.ds(F * M + M, M), :]
        mine_x.append(jnp.where(odd, first, last))
        mine_y.append(jnp.where(odd, last, first))

    def complete(t, parts):
        row, col, kind = t[ROW : ROW + 1], t[COL : COL + 1], t[KIND : KIND + 1]
        at = group.astype(f32) * C + kind * R + row
        total = jnp.zeros((M, C), f32)
        for packs, edge in parts:
            total += pickup(packs, jnp.where((group < 3) & (col == edge), at, -1.0))
        coef = jnp.where(col == 0.0, t[AW : AW + 1], t[AE : AE + 1])
        return t[:M] + coef * total

    def packs(got):
        return [got[pl.ds(n * M, M), :] for n in range(3)]

    for side, got in enumerate((got_x, got_y)):
        sides[side, :M] = sum(
            pltpu.roll(spare_only(h), C - SPARE + n * K, 1) for n, h in enumerate(packs(got))
        )
        sides[side, M:] = got[pl.ds(3 * M, T - M), :]
    out = []
    later = None
    for index, (src, parts) in enumerate((
        (own_in, ((packs(got_x), edge_x), (packs(got_y), edge_y))),
        (sides.at[0], ((mine_x, edge_y),)),
        (sides.at[1], ((mine_y, edge_x),)),
    )):
        raw = src
        t = raw[...]
        whole = jnp.concatenate([complete(t, parts), t[M:]], axis=0)
        if index == 0:
            later = whole
        out.append(choose(index, raw, *statistics(whole)))
    fields = jnp.concatenate([a for a, _ in out], axis=1)
    rank, count = ranks([a for _, a in out])
    rank = jnp.concatenate(rank, axis=1)
    count_out[0] = count
    compact_all(fields, rank, count, ycat, bcat, locs)

    prior = later[:M]
    row, col = later[ROW : ROW + 1], later[COL : COL + 1]

    def point(j, add):
        lw = taper(locs[j, 0] - row) * taper(locs[j, 1] - col) * locs[j, 2]
        return add + update(prior, lw, ycat[j], bcat[j])

    add = lax.fori_loop(0, jnp.maximum((count + S - 1) // S, 1), point, jnp.zeros((M, C), f32))
    later = jnp.concatenate([prior + add, later[M:]], axis=0)
    yp, gain, innov, alpha = statistics(later)
    fresh = stack_fields(yp, (gain, innov, alpha, row, col))
    fresh = jnp.concatenate([fresh, later[LIST:]], axis=0)
    lane = lanes((T, C))
    fresh = jnp.where((lane >= LATER) & (lane < LATER + K), fresh, 0.0)
    table[...] = pltpu.roll(fresh, C - LATER, 1)


def combine_kernel(own, a, b, out):
    out[...] = combine(own[...], a[...], b[...])


def advect_kernel(xt, got_a, got_b, cc, cr, state, edge):
    lane1 = lanes((1, C))
    odd_a = flag(parity("lat"), (M, C))

    def one(i, low, high):
        here, ae, aw, an, as_ = stencil(cc[0, pl.ds(i, 1), :], cr[0, pl.ds(i, 1), :])
        edge[pl.ds(i, 1), :] = jnp.where(
            lane1 == 0, aw, jnp.where(lane1 == C - 1, ae, 0.0)
        )
        ae = jnp.where(lane1 == C - 1, 0.0, ae)
        aw = jnp.where(lane1 == 0, 0.0, aw)
        for f in range(F):
            x = xt[f, i]
            ha, hb = got_a[pl.ds(f * M, M), :], got_b[pl.ds(f * M, M), :]
            xs = jnp.where(odd_a, ha, hb) if low else xt[f, i - 1]
            xn = jnp.where(odd_a, hb, ha) if high else xt[f, i + 1]
            y = here * x + ae * pltpu.roll(x, C - 1, 1) + aw * pltpu.roll(x, 1, 1)
            state[f, i] = y + an * xn + as_ * xs

    one(0, True, False)
    one(R - 1, False, True)

    def body(n, carry):
        one(2 * n + 1, False, False)
        one(2 * n + 2, False, False)
        return carry

    lax.fori_loop(0, R // 2 - 1, body, 0)


def lay_halos(got_x, got_y, merged):
    odd_lane = (lanes((M, C)) % 2) == 1
    odd_b = flag(parity("lon"), (M, C))
    got_1, got_2 = got_x[pl.ds(0, M), :], got_y[pl.ds(0, M), :]
    east = pltpu.roll(jnp.where(odd_b, got_2, got_1), C - 1, 1)
    west = jnp.where(odd_b, got_1, got_2)
    merged[0] = jnp.where(odd_lane, east, west)
    merged[1] = jnp.where(odd_lane, west, east)


def sweeps(row_of, count, ycat, bcat, locs, row_w, col_w, total, emit):
    def weigh(j):
        row_w[...] = taper(locs[j, 0] - lanes((S, C)).astype(f32))
        col_w[...] = taper(locs[j, 1] - lanes((S, C)).astype(f32)) * locs[j, 2]

    def sweep(base, j, put):
        def local(i):
            if isinstance(i, int):
                return jnp.broadcast_to(row_w[:, i : i + 1], (S, C)) * col_w[...]
            return taper(locs[j, 0] - i.astype(f32)) * col_w[...]

        def body(step, carry):
            for n in [step * STEP + u for u in range(STEP)]:
                i = 2 * n
                lw = jnp.concatenate([local(i), local(i + 1)], axis=1)
                for f in range(F):
                    pair = row_of(f, i, 0), row_of(f, i + 1, 1)
                    d = update(jnp.concatenate(pair, axis=1), lw, ycat[j], bcat[j])
                    if base is not None:
                        pair = base[f, i], base[f, i + 1]
                    put(n, f, pair[0] + d[:, :C], pair[1] + d[:, C:])
            return carry

        return body

    def keep(n, f, a, b):
        total[f, 2 * n] = a
        total[f, 2 * n + 1] = b

    @pl.when(count > S)
    def _():
        weigh(1)
        lax.fori_loop(0, R // 2 // STEP, sweep(None, 1, keep), 0)

        @pl.when(count > 2 * S)
        def _():
            weigh(2)
            lax.fori_loop(0, R // 2 // STEP, sweep(total, 2, keep), 0)

        weigh(0)
        emit(sweep, total)

    @pl.when(count <= S)
    def _():
        weigh(0)
        emit(sweep, None)


def first_kernel(count, state, edge, got_x, got_y, ycat, bcat, locs, out, row_w, col_w, total, merged):
    lay_halos(got_x, got_y, merged)

    def row_of(f, i, odd):
        halo = pltpu.roll(merged[odd], lax.rem(2 * C - (f * R + i), C), 1)
        return state[f, i] + halo * edge[pl.ds(i, 1), :]

    def emit(sweep, base):
        def put(n, f, a, b):
            out[f, 2 * n] = a
            out[f, 2 * n + 1] = b

        lax.fori_loop(0, R // 2 // STEP, sweep(base, 0, put), 0)

    sweeps(row_of, count[0], ycat, bcat, locs, row_w, col_w, total, emit)


def second_kernel(own, got_x, got_y, state, out, buf, sem, ycat, bcat, locs, row_w, col_w, total):
    parts = []
    for index, raw in enumerate((own, got_x, got_y)):
        t = raw[...]
        rows = (t[GAIN : GAIN + 1], t[INNOV : INNOV + 1], t[ALPHA : ALPHA + 1])
        parts.append(choose(index, raw, t[:M], *rows))
    rank, count = ranks([a for _, a in parts])
    fields = jnp.concatenate([a for a, _ in parts], axis=1)
    compact_all(fields, jnp.concatenate(rank, axis=1), count, ycat, bcat, locs)

    def copy(ib, f):
        return pltpu.make_async_copy(
            buf.at[ib, f], out.at[f, :, pl.ds(ib * 8, 8), :], sem.at[ib, f]
        )

    def emit(sweep, base):
        for ib in range(R // 8):

            def put(n, f, a, b):
                rows = buf.at[ib, f].reshape(M * 8, C)
                r = 2 * (n - 4 * ib)
                rows[pl.ds(r, M, stride=8), :] = a
                rows[pl.ds(r + 1, M, stride=8), :] = b

            for step in range(4 * ib // STEP, (4 * ib + 4) // STEP):
                sweep(base, 0, put)(step, 0)
            for f in range(F):
                copy(ib, f).start()

    sweeps(lambda f, i, odd: state[f, i], count, ycat, bcat, locs, row_w, col_w, total, emit)
    for ib in range(R // 8):
        for f in range(F):
            copy(ib, f).wait()


def call(kernel, outs, args, scratch=(), scalars=0, hbm=(), out_spaces=None, us=2, limit=24, pinned=()):
    spaces = [
        pltpu.SMEM if n < scalars else pltpu.HBM if n in hbm else VMEM for n in range(len(args))
    ]
    args = [
        pltpu.with_memory_space_constraint(a, s) if a.size > 100000 or s == pltpu.HBM or n in pinned else a
        for n, (a, s) in enumerate(zip(args, spaces))
    ]
    out_spaces = out_spaces or [VMEM] * len(outs)
    return pl.pallas_call(
        kernel,
        out_shape=outs,
        in_specs=[pl.BlockSpec(memory_space=s) for s in spaces],
        out_specs=[pl.BlockSpec(memory_space=s) for s in out_spaces],
        scratch_shapes=scratch,
        compiler_params=pltpu.CompilerParams(vmem_limit_bytes=limit * MiB),
        cost_estimate=pl.CostEstimate(flops=0, transcendentals=0, bytes_accessed=us * 3000000),
        name=kernel.__name__,
    )(*args)


def swap(x, axis, shift):
    n = lax.axis_size(axis)
    pairs = [(i, ((i - shift) ^ 1) + shift) for i in range(n)]
    pairs = [(i, j) for i, j in pairs if i >= shift and 0 <= j < n]
    return lax.ppermute(x, axis, pairs)


def on_device(
    ensemble, courant_cols, courant_rows, obs_value, obs_error, obs_cell, obs_kind, obs_live, obs_list
):
    listed = jnp.transpose(obs_list, (2, 0, 1))
    block = VMEM((F, R, M, C), f32)
    sds = jax.ShapeDtypeStruct
    copies = [VMEM((R // 8, F, M, 8, C), f32)]
    sems = pltpu.SemaphoreType.DMA((R // 8, F))

    small = [
        obs_cell, obs_kind, courant_cols, courant_rows, obs_value, obs_error, obs_live, listed
    ]
    held = [(pltpu.SMEM if n < 2 else VMEM)(a.shape, a.dtype) for n, a in enumerate(small)]
    held_sems = pltpu.SemaphoreType.DMA((len(small),))

    pay_shape = sds((4 * M + T, C), f32)
    xt, pay_a, pay_b, *held = call(
        edges_kernel,
        [block, pay_shape, pay_shape, *held],
        [ensemble, *small],
        [*copies, VMEM((3, T, C), f32), sems, held_sems],
        hbm=range(9),
        out_spaces=[VMEM] * 3 + [pltpu.SMEM] * 2 + [VMEM] * 6,
    )
    got_b, got_a = swap(pay_b, "lat", 1), swap(pay_a, "lat", 0)
    later = call(
        later_kernel, [sds((T, C), f32)], [*held[:2], xt, *held[2:]], scalars=2, us=1, pinned=range(9)
    )[0]
    lon_shape = sds((2 * M + T, C), f32)
    out_a, out_b, own = call(
        rows_kernel, [lon_shape] * 2 + [sds((T, C), f32)], [xt, pay_a, later, got_a, got_b]
    )
    got_y, got_x = swap(out_b, "lon", 1), swap(out_a, "lon", 0)
    state, edge = call(
        advect_kernel,
        [block, sds((R, C), f32)],
        [xt, got_a, got_b, held[2], held[3]],
        pinned=(3, 4),
    )
    chosen = [sds((3, S, 2 * C), bf16), sds((3, M, 2 * C), bf16), sds((3, 3, S, C), f32)]
    table, count, *picked = call(
        tables_kernel,
        [sds((T, C), f32), sds((1,), jnp.int32), *chosen],
        [pay_a, got_a, got_b, own, got_x, got_y, edge],
        [VMEM((2, T, C), f32)],
        out_spaces=[VMEM, pltpu.SMEM, VMEM, VMEM, VMEM],
    )
    tab_b, tab_a = swap(table, "lat", 1), swap(table, "lat", 0)
    column = call(combine_kernel, [sds((T, C), f32)], [table, tab_a, tab_b], us=1)[0]
    col_y, col_x = swap(column, "lon", 1), swap(column, "lon", 0)
    work = [VMEM((S, C), f32), VMEM((S, C), f32), VMEM((F, R, M, C), f32)]
    state = call(
        first_kernel,
        [block],
        [count, state, edge, got_x, got_y, *picked],
        work + [VMEM((2, M, C), f32)],
        scalars=1,
        us=4,
    )[0]
    return call(
        second_kernel,
        [sds((F, M, R, C), f32)],
        [column, col_x, col_y, state],
        [*copies, sems]
        + [VMEM((3, S, 2 * C), bf16), VMEM((3, M, 2 * C), bf16), VMEM((3, 3, S, C), f32)]
        + work,
        out_spaces=[pltpu.HBM],
        us=6,
    )[0]


def solution(mesh):
    tiles = P(None, ("lat", "lon"))
    placed = (
        P(None, None, "lat", "lon"),
        P(None, "lat", "lon"),
        P(None, "lat", "lon"),
        tiles,
        tiles,
        tiles,
        tiles,
        tiles,
        P(None, ("lat", "lon"), None),
    )
    return jax.shard_map(
        on_device,
        mesh=mesh,
        in_specs=placed,
        out_specs=P(None, None, "lat", "lon"),
        check_vma=False,
    )
```

```python
import jax
import jax.numpy as jnp
from jax import lax
from jax.experimental import pallas as pl
from jax.experimental.pallas import tpu as pltpu
from jax.sharding import PartitionSpec as P

F, M, R, C, K = 3, 80, 32, 128, 24
GAIN, INNOV, ALPHA, ROW, COL, KIND = 80, 81, 82, 83, 84, 85
AE, AW, AN, AS, LIST, T = 88, 89, 90, 91, 96, 112
VALUE, ERROR, LIVE = GAIN, INNOV, ALPHA
SPARE = 96
LATER = 96
S = 80
STEP = 4
f32, bf16 = jnp.float32, jnp.bfloat16
VMEM = pltpu.VMEM
MiB = 1 << 20


def lanes(shape):
    return lax.broadcasted_iota(jnp.int32, shape, len(shape) - 1)


def split(x):
    hi = x.astype(bf16)
    return hi, (x - hi.astype(f32)).astype(bf16)


def dot(a, b, dims=((1,), (0,))):
    return lax.dot_general(a, b, (dims, ((), ())), preferred_element_type=f32)


def subs(shape):
    return lax.broadcasted_iota(jnp.int32, shape, 0)


def parity(axis):
    return lax.rem(lax.axis_index(axis), 2)


def flag(value, shape):
    return (jnp.zeros(shape, jnp.int32) + value) == 1


def stencil(u, v):
    uu, vv = 0.5 * u * u, 0.5 * v * v
    return 1.0 - 2.0 * uu - 2.0 * vv, uu - 0.5 * u, uu + 0.5 * u, vv - 0.5 * v, vv + 0.5 * v


def own_part(b, start, xt, cell, kind, cc, cr, value, error, live, listed, cells, kinds, part):
    lane, lane1, lane8 = lanes((M, C)), lanes((1, C)), lanes((8, C))
    sub8 = subs((8, C))
    zero = jnp.zeros((1, C), f32)
    prior = jnp.zeros((M, C), f32)
    coefs = jnp.zeros((8, C), f32)
    for s in range(K):
        at = cell[b, s]
        r, c = lax.shift_right_logical(at, 7), lax.bitwise_and(at, C - 1)
        f = kind[b, s]
        here, ae, aw, an, as_ = (
            jnp.where(lane1 == c, w, 0.0)
            for w in stencil(cc[0, pl.ds(r, 1), :], cr[0, pl.ds(r, 1), :])
        )
        stack = jnp.where(
            sub8 == 0, ae, jnp.where(sub8 == 1, aw, jnp.where(sub8 == 2, an, as_))
        )
        total = jnp.sum(stack, axis=1, keepdims=True)
        coefs = jnp.where(lane8 == start + s, total, coefs)
        ae = pltpu.roll(jnp.where(lane1 == C - 1, 0.0, ae), 1, 1)
        aw = pltpu.roll(jnp.where(lane1 == 0, 0.0, aw), C - 1, 1)
        an = jnp.where(r == R - 1, zero, an)
        as_ = jnp.where(r == 0, zero, as_)
        y = (here + ae + aw) * xt[f, r]
        y = y + an * xt[f, jnp.minimum(r + 1, R - 1)] + as_ * xt[f, jnp.maximum(r - 1, 0)]
        prior = jnp.where(lane == start + s, jnp.sum(y, axis=1, keepdims=True), prior)
    part[...] = jnp.zeros((T, C), f32)
    part[:M] = prior
    part[AE : AE + 8, :] = coefs
    keep = slice(start, start + K)
    at = cells[b : b + 1, :]
    part[ROW : ROW + 1, keep] = lax.shift_right_logical(at, 7).astype(f32)
    part[COL : COL + 1, keep] = lax.bitwise_and(at, C - 1).astype(f32)
    part[KIND : KIND + 1, keep] = kinds[b : b + 1, :].astype(f32)
    part[VALUE : VALUE + 1, keep] = value[b : b + 1, :]
    part[ERROR : ERROR + 1, keep] = error[b : b + 1, :]
    part[LIVE : LIVE + 1, keep] = live[b : b + 1, :].astype(f32)
    for n in range(9):
        part[LIST + n : LIST + n + 1, keep] = listed[n, b : b + 1, :].astype(f32)


def small_copies(srcs, dsts, sems):
    return [pltpu.make_async_copy(a, b, sems.at[n]) for n, (a, b) in enumerate(zip(srcs, dsts))]


def edges_kernel(*refs):
    x_hbm, small = refs[0], refs[1:11]
    xt, pay_a, pay_b = refs[11:14]
    here = refs[14:24]
    buf, acc, sem, small_sem = refs[24:]
    for ib in range(R // 8):
        for f in range(F):
            pltpu.make_async_copy(
                x_hbm.at[f, :, pl.ds(ib * 8, 8), :], buf.at[ib, f], sem.at[ib, f]
            ).start()
    copies = small_copies(small, here, small_sem)
    for c in copies:
        c.start()
    acc[...] = jnp.zeros_like(acc)
    lane = lanes((M, C))
    for ib in range(R // 8):
        for f in range(F):
            pltpu.make_async_copy(
                x_hbm.at[f, :, pl.ds(ib * 8, 8), :], buf.at[ib, f], sem.at[ib, f]
            ).wait()
            rows = buf.at[ib, f].reshape(M * 8, C)
            first, last = acc[0, :M], acc[1, :M]
            for r in range(8):
                v = rows[pl.ds(r, M, stride=8), :]
                i = ib * 8 + r
                k = f * R + i
                xt[f, i] = v
                turned = pltpu.roll(v, k, 1) if k else v
                first = jnp.where(lane == k, turned, first)
                last = jnp.where(lane == (k - 1) % C, turned, last)
            acc[0, :M] = first
            acc[1, :M] = last
    first, last = acc[0, :M], pltpu.roll(acc[1, :M], 1, 1)
    ra = jnp.where(parity("lat") == 1, 0, R - 1)
    rb = R - 1 - ra
    for f in range(F):
        pay_a[pl.ds(f * M, M), :] = xt[f, ra]
        pay_b[pl.ds(f * M, M), :] = xt[f, rb]
    for c in copies:
        c.wait()
    part = acc.at[2]
    own_part(0, SPARE, xt, *here, part)
    first = first + part[:M]
    for pay in (pay_a, pay_b):
        pay[pl.ds(F * M, M), :] = first
        pay[pl.ds(F * M + M, M), :] = last
        pay[pl.ds(5 * M, T - M), :] = part[M:]


def later_kernel(cell, kind, xt, *refs):
    own_part(1, LATER, xt, cell, kind, *refs)


def combine(own, a, b):
    few = lanes((T, C)) < K
    return (
        own
        + pltpu.roll(jnp.where(few, a, 0.0), K, 1)
        + pltpu.roll(jnp.where(few, b, 0.0), 2 * K, 1)
    )


def lane_group():
    lane = lanes((1, C))
    group = jnp.where(lane < 2 * K, 1, jnp.where(lane < 3 * K, 2, 3))
    return jnp.where((lane < K) | ((lane >= LATER) & (lane < LATER + K)), 0, group)


def pickup(sources, key):
    hot = (subs((F * C, C)).astype(f32) == key).astype(f32).astype(bf16)
    return sum(dot(h, hot) for h in split(jnp.concatenate(sources, axis=1)))


def spare_only(x):
    lane = lanes(x.shape)
    return jnp.where((lane >= SPARE) & (lane < SPARE + K), x, 0.0)


def rows_kernel(xt, pay, later, got_a, got_b, out_a, out_b, own):
    pa, pb = parity("lat"), parity("lon")
    comb = later[...]
    for n, src in enumerate((pay, got_a, got_b)):
        part = jnp.concatenate([src[pl.ds(F * M, M), :], src[pl.ds(5 * M, T - M), :]], axis=0)
        comb = comb + pltpu.roll(spare_only(part), C - SPARE + n * K, 1)
    row, col, kind = comb[ROW : ROW + 1], comb[COL : COL + 1], comb[KIND : KIND + 1]
    group = lane_group()
    edge_a = jnp.where(pa == 1, 0, R - 1)
    edge_b = R - 1 - edge_a
    cellkey = kind * C + col

    def key(n, edge):
        return jnp.where((group == n) & (row == edge.astype(f32)), cellkey, -1.0)

    total = pickup([got_a[pl.ds(f * M, M), :] for f in range(F)], key(0, edge_a))
    total += pickup([got_b[pl.ds(f * M, M), :] for f in range(F)], key(0, edge_b))
    total += pickup([xt[f, edge_a] for f in range(F)], key(1, edge_b))
    total += pickup([xt[f, edge_b] for f in range(F)], key(2, edge_a))
    coef = jnp.where(row == 0.0, comb[AS : AS + 1], comb[AN : AN + 1])
    prior = comb[:M] + coef * total
    odd = flag(pb, (M, C))
    for n, src in enumerate((pay, got_a, got_b)):
        first, last = src[pl.ds(F * M, M), :], src[pl.ds(F * M + M, M), :]
        column = lanes((M, C)) < SPARE
        mine = spare_only(pltpu.roll(prior, SPARE - n * K, 1))
        out_a[pl.ds(n * M, M), :] = jnp.where(column, jnp.where(odd, first, last), mine)
        out_b[pl.ds(n * M, M), :] = jnp.where(column, jnp.where(odd, last, first), mine)
    for out in (out_a, out_b):
        out[pl.ds(3 * M, T - M), :] = comb[M:]
    own[:M] = prior
    own[M:] = comb[M:]


def statistics(t):
    prior = t[:M]
    ybar = jnp.sum(prior, axis=0, keepdims=True) / M
    yp = prior - ybar
    spread = jnp.sum(yp * yp, axis=0, keepdims=True) / (M - 1)
    err = t[ERROR : ERROR + 1]
    total = spread + err
    total = jnp.where(total == 0.0, 1.0, total)
    gain = t[LIVE : LIVE + 1] / total
    alpha = 1.0 / (1.0 + jnp.sqrt(err / total))
    innov = t[VALUE : VALUE + 1] - ybar
    return yp, gain, innov, alpha


def stack_fields(yp, rows):
    sub = subs((16, C))
    extra = jnp.zeros((16, C), f32)
    for n, v in enumerate(rows):
        extra = jnp.where(sub == n, v, extra)
    return jnp.concatenate([yp, extra], axis=0)


def choose(index, raw, yp, gain, innov, alpha):
    sa = 1 - 2 * parity("lat")
    sb = 1 - 2 * parity("lon")
    db = (0, sb, -sb)[index]
    group = lane_group()
    chosen = jnp.zeros((1, C), f32)
    row = raw[ROW : ROW + 1, :]
    for n, da in enumerate((0, sa, -sa)):
        listed = raw[pl.ds(LIST + (1 - da) * 3 + (1 - db), 1), :]
        chosen = jnp.where(group == n, listed, chosen)
        row = jnp.where(group == n, row + jnp.asarray(da * R, f32), row)
    col = raw[COL : COL + 1, :] + jnp.asarray(db * C, f32)
    factor = gain * chosen
    near = (row > -float(R)) & (row < 2.0 * R - 1.0) & (col > -float(R)) & (col < C + R - 1.0)
    act = near & (factor != 0.0) & (lanes((1, C)) < 3 * K)
    return stack_fields(yp, (factor, innov, alpha, row, col)), jnp.where(act, 1.0, 0.0)


def ranks(actives):
    before = (subs((C, C)) < lanes((C, C))).astype(f32).astype(bf16)
    out, offset = [], jnp.zeros((1, 1), f32)
    for act in actives:
        r = dot(jnp.broadcast_to(act, (8, C)).astype(bf16), before)[:1] + offset
        out.append(jnp.where(act > 0.0, r, -1.0))
        offset = offset + jnp.sum(act, axis=1, keepdims=True)
    return out, sum(jnp.sum(a) for a in actives).astype(jnp.int32)


def spread_lanes(hi, lo):
    r = lax.broadcasted_iota(jnp.int32, (C, 2 * C), 0)
    c = lax.broadcasted_iota(jnp.int32, (C, 2 * C), 1)
    keep = r < S
    e_hi = (((c == r) | (c == r + 2 * S)) & keep).astype(f32).astype(bf16)
    e_lo = ((c == r + S) & keep).astype(f32).astype(bf16)
    return (dot(hi, e_hi) + dot(lo, e_lo)).astype(bf16)


def compact(fields, rank, chunk, ycat, bcat, locs):
    p = subs((C, F * C)).astype(f32) + jnp.asarray(chunk * S, f32)
    own = subs((C, F * C)) < S
    pick = ((rank == p) & own).astype(f32).astype(bf16)
    turned = sum(dot(t, pick, ((1,), (1,))) for t in split(fields))
    chosen = jnp.concatenate([turned, jnp.zeros((32, C), f32)], axis=0).T[:S]
    ycat[chunk] = spread_lanes(*split(chosen))
    back = turned[INNOV : INNOV + 1, :] - turned[ALPHA : ALPHA + 1, :] * turned[:M]
    bcat[chunk] = spread_lanes(*split(back))
    locs[chunk, 0] = jnp.broadcast_to(chosen[:, ROW : ROW + 1], (S, C))
    locs[chunk, 1] = jnp.broadcast_to(chosen[:, COL : COL + 1], (S, C))
    locs[chunk, 2] = jnp.broadcast_to(chosen[:, GAIN : GAIN + 1], (S, C)) / (M - 1)


def compact_all(fields, rank, count, ycat, bcat, locs):
    compact(fields, rank, 0, ycat, bcat, locs)

    @pl.when(count > S)
    def _():
        def body(j, carry):
            compact(fields, rank, j, ycat, bcat, locs)
            return carry

        lax.fori_loop(1, (count + S - 1) // S, body, 0)


def taper(d):
    z = jnp.maximum(0.0, 1.0 - jnp.abs(d) / R)
    return z * z


def update(p, lw, ycat, bcat):
    hi, lo = split(p)
    none = jnp.zeros((2 * C - 3 * M, p.shape[1]), bf16)
    proj = dot(ycat, jnp.concatenate([hi, hi, lo, none], axis=0))
    hi, lo = split(proj * lw)
    return dot(bcat, jnp.concatenate([hi, hi, lo, none], axis=0))


def tables_kernel(
    pay, got_a, got_b, own_in, got_x, got_y, after, table, count_out, ycat, bcat, locs, sides
):
    pb = parity("lon")
    edge_x = jnp.where(pb == 1, 0.0, C - 1.0)
    edge_y = C - 1.0 - edge_x
    group = lane_group()
    odd = flag(pb, (M, C))
    mine_x, mine_y = [], []
    for src in (pay, got_a, got_b):
        first, last = src[pl.ds(F * M, M), :], src[pl.ds(F * M + M, M), :]
        mine_x.append(jnp.where(odd, first, last))
        mine_y.append(jnp.where(odd, last, first))

    def complete(t, parts):
        row, col, kind = t[ROW : ROW + 1], t[COL : COL + 1], t[KIND : KIND + 1]
        at = group.astype(f32) * C + kind * R + row
        total = jnp.zeros((M, C), f32)
        for packs, edge in parts:
            total += pickup(packs, jnp.where((group < 3) & (col == edge), at, -1.0))
        coef = jnp.where(col == 0.0, t[AW : AW + 1], t[AE : AE + 1])
        return t[:M] + coef * total

    def packs(got):
        return [got[pl.ds(n * M, M), :] for n in range(3)]

    for side, got in enumerate((got_x, got_y)):
        sides[side, :M] = sum(
            pltpu.roll(spare_only(h), C - SPARE + n * K, 1) for n, h in enumerate(packs(got))
        )
        sides[side, M:] = got[pl.ds(3 * M, T - M), :]
    out = []
    later = None
    for index, (src, parts) in enumerate((
        (own_in, ((packs(got_x), edge_x), (packs(got_y), edge_y))),
        (sides.at[0], ((mine_x, edge_y),)),
        (sides.at[1], ((mine_y, edge_x),)),
    )):
        raw = src
        t = raw[...]
        whole = jnp.concatenate([complete(t, parts), t[M:]], axis=0)
        if index == 0:
            later = whole
        out.append(choose(index, raw, *statistics(whole)))
    fields = jnp.concatenate([a for a, _ in out], axis=1)
    rank, count = ranks([a for _, a in out])
    rank = jnp.concatenate(rank, axis=1)
    count_out[0] = count
    compact_all(fields, rank, count, ycat, bcat, locs)

    prior = later[:M]
    row, col = later[ROW : ROW + 1], later[COL : COL + 1]

    def point(j, add):
        lw = taper(locs[j, 0] - row) * taper(locs[j, 1] - col) * locs[j, 2]
        return add + update(prior, lw, ycat[j], bcat[j])

    add = lax.fori_loop(0, jnp.maximum((count + S - 1) // S, 1), point, jnp.zeros((M, C), f32))
    later = jnp.concatenate([prior + add, later[M:]], axis=0)
    yp, gain, innov, alpha = statistics(later)
    fresh = stack_fields(yp, (gain, innov, alpha, row, col))
    fresh = jnp.concatenate([fresh, later[LIST:]], axis=0)
    lane = lanes((T, C))
    fresh = jnp.where((lane >= LATER) & (lane < LATER + K), fresh, 0.0)
    table[...] = pltpu.roll(fresh, C - LATER, 1)


def combine_kernel(own, a, b, out):
    out[...] = combine(own[...], a[...], b[...])


def advect_kernel(xt, got_a, got_b, cc, cr, state, edge):
    lane1 = lanes((1, C))
    odd_a = flag(parity("lat"), (M, C))

    def one(i, low, high):
        here, ae, aw, an, as_ = stencil(cc[0, pl.ds(i, 1), :], cr[0, pl.ds(i, 1), :])
        edge[pl.ds(i, 1), :] = jnp.where(
            lane1 == 0, aw, jnp.where(lane1 == C - 1, ae, 0.0)
        )
        ae = jnp.where(lane1 == C - 1, 0.0, ae)
        aw = jnp.where(lane1 == 0, 0.0, aw)
        for f in range(F):
            x = xt[f, i]
            ha, hb = got_a[pl.ds(f * M, M), :], got_b[pl.ds(f * M, M), :]
            xs = jnp.where(odd_a, ha, hb) if low else xt[f, i - 1]
            xn = jnp.where(odd_a, hb, ha) if high else xt[f, i + 1]
            y = here * x + ae * pltpu.roll(x, C - 1, 1) + aw * pltpu.roll(x, 1, 1)
            state[f, i] = y + an * xn + as_ * xs

    one(0, True, False)
    one(R - 1, False, True)

    def body(n, carry):
        one(2 * n + 1, False, False)
        one(2 * n + 2, False, False)
        return carry

    lax.fori_loop(0, R // 2 - 1, body, 0)


def lay_halos(got_x, got_y, merged):
    odd_lane = (lanes((M, C)) % 2) == 1
    odd_b = flag(parity("lon"), (M, C))
    got_1, got_2 = got_x[pl.ds(0, M), :], got_y[pl.ds(0, M), :]
    east = pltpu.roll(jnp.where(odd_b, got_2, got_1), C - 1, 1)
    west = jnp.where(odd_b, got_1, got_2)
    merged[0] = jnp.where(odd_lane, east, west)
    merged[1] = jnp.where(odd_lane, west, east)


def sweeps(row_of, count, ycat, bcat, locs, row_w, col_w, total, emit):
    def weigh(j):
        row_w[...] = taper(locs[j, 0] - lanes((S, C)).astype(f32))
        col_w[...] = taper(locs[j, 1] - lanes((S, C)).astype(f32)) * locs[j, 2]

    def sweep(base, j, put):
        def local(i):
            if isinstance(i, int):
                return jnp.broadcast_to(row_w[:, i : i + 1], (S, C)) * col_w[...]
            return taper(locs[j, 0] - i.astype(f32)) * col_w[...]

        def body(step, carry):
            for n in [step * STEP + u for u in range(STEP)]:
                i = 2 * n
                lw = jnp.concatenate([local(i), local(i + 1)], axis=1)
                for f in range(F):
                    pair = row_of(f, i, 0), row_of(f, i + 1, 1)
                    d = update(jnp.concatenate(pair, axis=1), lw, ycat[j], bcat[j])
                    if base is not None:
                        pair = base[f, i], base[f, i + 1]
                    put(n, f, pair[0] + d[:, :C], pair[1] + d[:, C:])
            return carry

        return body

    def keep(n, f, a, b):
        total[f, 2 * n] = a
        total[f, 2 * n + 1] = b

    @pl.when(count > S)
    def _():
        weigh(1)
        lax.fori_loop(0, R // 2 // STEP, sweep(None, 1, keep), 0)

        @pl.when(count > 2 * S)
        def _():
            weigh(2)
            lax.fori_loop(0, R // 2 // STEP, sweep(total, 2, keep), 0)

        weigh(0)
        emit(sweep, total)

    @pl.when(count <= S)
    def _():
        weigh(0)
        emit(sweep, None)


def first_kernel(count, state, edge, got_x, got_y, ycat, bcat, locs, out, row_w, col_w, total, merged):
    lay_halos(got_x, got_y, merged)

    def row_of(f, i, odd):
        halo = pltpu.roll(merged[odd], lax.rem(2 * C - (f * R + i), C), 1)
        return state[f, i] + halo * edge[pl.ds(i, 1), :]

    def emit(sweep, base):
        def put(n, f, a, b):
            out[f, 2 * n] = a
            out[f, 2 * n + 1] = b

        lax.fori_loop(0, R // 2 // STEP, sweep(base, 0, put), 0)

    sweeps(row_of, count[0], ycat, bcat, locs, row_w, col_w, total, emit)


def second_kernel(own, got_x, got_y, state, out, buf, sem, ycat, bcat, locs, row_w, col_w, total):
    parts = []
    for index, raw in enumerate((own, got_x, got_y)):
        t = raw[...]
        rows = (t[GAIN : GAIN + 1], t[INNOV : INNOV + 1], t[ALPHA : ALPHA + 1])
        parts.append(choose(index, raw, t[:M], *rows))
    rank, count = ranks([a for _, a in parts])
    fields = jnp.concatenate([a for a, _ in parts], axis=1)
    compact_all(fields, jnp.concatenate(rank, axis=1), count, ycat, bcat, locs)

    def copy(ib, f):
        return pltpu.make_async_copy(
            buf.at[ib, f], out.at[f, :, pl.ds(ib * 8, 8), :], sem.at[ib, f]
        )

    def emit(sweep, base):
        for ib in range(R // 8):

            def put(n, f, a, b):
                rows = buf.at[ib, f].reshape(M * 8, C)
                r = 2 * (n - 4 * ib)
                rows[pl.ds(r, M, stride=8), :] = a
                rows[pl.ds(r + 1, M, stride=8), :] = b

            for step in range(4 * ib // STEP, (4 * ib + 4) // STEP):
                sweep(base, 0, put)(step, 0)
            for f in range(F):
                copy(ib, f).start()

    sweeps(lambda f, i, odd: state[f, i], count, ycat, bcat, locs, row_w, col_w, total, emit)
    for ib in range(R // 8):
        for f in range(F):
            copy(ib, f).wait()


def call(kernel, outs, args, scratch=(), scalars=0, hbm=(), out_spaces=None, us=2, limit=24, pinned=()):
    spaces = [
        pltpu.SMEM if n < scalars else pltpu.HBM if n in hbm else VMEM for n in range(len(args))
    ]
    args = [
        pltpu.with_memory_space_constraint(a, s) if a.size > 100000 or s == pltpu.HBM or n in pinned else a
        for n, (a, s) in enumerate(zip(args, spaces))
    ]
    out_spaces = out_spaces or [VMEM] * len(outs)
    return pl.pallas_call(
        kernel,
        out_shape=outs,
        in_specs=[pl.BlockSpec(memory_space=s) for s in spaces],
        out_specs=[pl.BlockSpec(memory_space=s) for s in out_spaces],
        scratch_shapes=scratch,
        compiler_params=pltpu.CompilerParams(vmem_limit_bytes=limit * MiB),
        cost_estimate=pl.CostEstimate(flops=0, transcendentals=0, bytes_accessed=us * 3000000),
        name=kernel.__name__,
    )(*args)


def swap(x, axis, shift):
    n = lax.axis_size(axis)
    pairs = [(i, ((i - shift) ^ 1) + shift) for i in range(n)]
    pairs = [(i, j) for i, j in pairs if i >= shift and 0 <= j < n]
    return lax.ppermute(x, axis, pairs)


def on_device(
    ensemble, courant_cols, courant_rows, obs_value, obs_error, obs_cell, obs_kind, obs_live, obs_list
):
    listed = jnp.transpose(obs_list, (2, 0, 1))
    block = VMEM((F, R, M, C), f32)
    sds = jax.ShapeDtypeStruct
    copies = [VMEM((R // 8, F, M, 8, C), f32)]
    sems = pltpu.SemaphoreType.DMA((R // 8, F))

    small = [
        obs_cell, obs_kind, courant_cols, courant_rows, obs_value, obs_error, obs_live, listed,
        obs_cell, obs_kind,
    ]
    held = [(pltpu.SMEM if n < 2 else VMEM)(a.shape, a.dtype) for n, a in enumerate(small)]
    held_sems = pltpu.SemaphoreType.DMA((len(small),))

    pay_shape = sds((4 * M + T, C), f32)
    xt, pay_a, pay_b, *held = call(
        edges_kernel,
        [block, pay_shape, pay_shape, *held],
        [ensemble, *small],
        [*copies, VMEM((3, T, C), f32), sems, held_sems],
        hbm=range(11),
        out_spaces=[VMEM] * 3 + [pltpu.SMEM] * 2 + [VMEM] * 8,
    )
    got_b, got_a = swap(pay_b, "lat", 1), swap(pay_a, "lat", 0)
    later = call(
        later_kernel, [sds((T, C), f32)], [*held[:2], xt, *held[2:]], scalars=2, us=1, pinned=range(11)
    )[0]
    lon_shape = sds((2 * M + T, C), f32)
    out_a, out_b, own = call(
        rows_kernel, [lon_shape] * 2 + [sds((T, C), f32)], [xt, pay_a, later, got_a, got_b]
    )
    got_y, got_x = swap(out_b, "lon", 1), swap(out_a, "lon", 0)
    state, edge = call(
        advect_kernel,
        [block, sds((R, C), f32)],
        [xt, got_a, got_b, held[2], held[3]],
        pinned=(3, 4),
    )
    chosen = [sds((3, S, 2 * C), bf16), sds((3, M, 2 * C), bf16), sds((3, 3, S, C), f32)]
    table, count, *picked = call(
        tables_kernel,
        [sds((T, C), f32), sds((1,), jnp.int32), *chosen],
        [pay_a, got_a, got_b, own, got_x, got_y, edge],
        [VMEM((2, T, C), f32)],
        out_spaces=[VMEM, pltpu.SMEM, VMEM, VMEM, VMEM],
    )
    tab_b, tab_a = swap(table, "lat", 1), swap(table, "lat", 0)
    column = call(combine_kernel, [sds((T, C), f32)], [table, tab_a, tab_b], us=1)[0]
    col_y, col_x = swap(column, "lon", 1), swap(column, "lon", 0)
    work = [VMEM((S, C), f32), VMEM((S, C), f32), VMEM((F, R, M, C), f32)]
    state = call(
        first_kernel,
        [block],
        [count, state, edge, got_x, got_y, *picked],
        work + [VMEM((2, M, C), f32)],
        scalars=1,
        us=4,
    )[0]
    return call(
        second_kernel,
        [sds((F, M, R, C), f32)],
        [column, col_x, col_y, state],
        [*copies, sems]
        + [VMEM((3, S, 2 * C), bf16), VMEM((3, M, 2 * C), bf16), VMEM((3, 3, S, C), f32)]
        + work,
        out_spaces=[pltpu.HBM],
        us=6,
    )[0]


def solution(mesh):
    tiles = P(None, ("lat", "lon"))
    placed = (
        P(None, None, "lat", "lon"),
        P(None, "lat", "lon"),
        P(None, "lat", "lon"),
        tiles,
        tiles,
        tiles,
        tiles,
        tiles,
        P(None, ("lat", "lon"), None),
    )
    return jax.shard_map(
        on_device,
        mesh=mesh,
        in_specs=placed,
        out_specs=P(None, None, "lat", "lon"),
        check_vma=False,
    )
```
